32 devices in a mesh: dp: 2 (over y), fsdp: 4 (over x, core), tensor: 4 (over z).
Axes of the slice: x: 2, y: 2, z: 4, core: 2. Of those that a mesh axis runs over, the one named last changes fastest.
Arguments:
- activations: bfloat16 [1024, 8192], P(('dp', 'fsdp'), 'tensor'), may hold values from -6 to 6
- cotangent: bfloat16 [1024, 8192], P(('dp', 'fsdp'), 'tensor'), may hold values from -6 to 6
- up_tiles: bfloat16 [1024, 128, 128], P(('fsdp', 'tensor')), may hold values from -0.1875 to 0.1875
- down_tiles: bfloat16 [1024, 128, 128], P(('fsdp', 'tensor')), may hold values from -0.125 to 0.125
- up_rows: int32 [256, 4], P(None, 'tensor'), may hold values from 0 to 63, as said below
- up_cols: int32 [256, 4], P(None, 'tensor'), may hold values from 0 to 31, as said below
- down_rows: int32 [256, 4], P(None, 'tensor'), may hold values from 0 to 31, as said below
- down_cols: int32 [256, 4], P(None, 'tensor'), may hold values from 0 to 63, as said below
Outputs:
- output: bfloat16 [1024, 8192], P(('dp', 'fsdp'), 'tensor')
- input_grad: bfloat16 [1024, 8192], P(('dp', 'fsdp'), 'tensor')
- up_grad: float32 [1024, 128, 128], P(('fsdp', 'tensor'))
- down_grad: float32 [1024, 128, 128], P(('fsdp', 'tensor'))
The draws below stay inside these ranges and needn't reach their ends.
Inputs may be any that keep to these rules, and one draw needn't show every extreme that they name: `up_rows`: within a column, the up tiles of one hidden-unit block name distinct feature blocks. `up_cols`: every value occurs exactly 8 times in each column. `down_rows`: every value occurs exactly 8 times in each column. `down_cols`: within a column, the down tiles of one hidden-unit block name distinct feature blocks.
All inputs are finite; a program needn't handle non-finite values.
Results may differ from the reference program's by a relative error of at most 0.018.
Values may be sent and summed in bfloat16 or wider, within the bound.
A program may use at most 128 MiB of HBM per device.

```python
import jax
import jax.numpy as jnp
from jax import lax

D = 8192
FF = 16384
BLOCK = 128
TOK_DEV = 128
TOKENS = 1024
RANK_COLS = 32
COL_TILES = 8
RANK_TILES = 256
TILES = 1024
TILE_DEV = 64
N_FSDP = 4
N_TENSOR = 4


def tile_lists(key):
    model_blocks = D // BLOCK
    ranks_here = TILES // RANK_TILES

    def one_block(block_key, top_here, bottom_here):
        order = jax.random.permutation(block_key, model_blocks).astype(jnp.int32)
        spots = jnp.arange(model_blocks, dtype=jnp.int32)
        top_spot = jnp.sum(jnp.where(order == model_blocks - 1, spots, 0))
        moved = order.at[top_spot].set(order[0]).at[0].set(model_blocks - 1)
        order = jnp.where(top_here, moved, order)
        low_spot = jnp.sum(jnp.where(order == 0, spots, 0))
        moved = order.at[low_spot].set(order[1]).at[1].set(0)
        order = jnp.where(bottom_here, moved, order)
        return order[:COL_TILES]

    def one_rank(rank_key):
        order_key, block_key, pick_key = jax.random.split(rank_key, 3)
        chosen = jax.random.randint(pick_key, (2,), 0, RANK_COLS)
        blocks = jnp.arange(RANK_COLS, dtype=jnp.int32)
        block_keys = jax.random.split(block_key, RANK_COLS)
        table = jax.vmap(one_block)(block_keys, blocks == chosen[0], blocks == chosen[1])
        slots = jax.random.permutation(order_key, RANK_TILES).astype(jnp.int32)
        near_blocks = slots // COL_TILES
        far_blocks = table[near_blocks, slots % COL_TILES]
        return (far_blocks, near_blocks)
    keys = jax.random.split(key, ranks_here)
    far_blocks, near_blocks = jax.vmap(one_rank)(keys)
    return (far_blocks.T.astype(jnp.int32), near_blocks.T.astype(jnp.int32))


def draw_up_rows(key, part):
    return tile_lists(jax.random.fold_in(key, 11))[0]


def draw_up_cols(key, part):
    return tile_lists(jax.random.fold_in(key, 11))[1]


def draw_down_rows(key, part):
    return tile_lists(jax.random.fold_in(key, 12))[1]


def draw_down_cols(key, part):
    return tile_lists(jax.random.fold_in(key, 12))[0]


def block_levels(rng, extent, shards, low, top_value):
    def one(dim, shards_of):
        draws = jax.random.uniform(jax.random.fold_in(jax.random.fold_in(rng, 6), dim), (shards_of,), jnp.float32, low / len(shards), top_value / len(shards))
        return jnp.repeat(jnp.exp(draws), extent[dim] // shards_of).reshape((-1,) + (1,) * (len(extent) - dim - 1))

    level = one(*shards[0])
    for cut in shards[1:]:
        level = level * one(*cut)
    return level


def normal_values(rng, shape, scale, most, cuts=(), kind=jnp.bfloat16):
    values = scale * jax.random.normal(rng, shape, jnp.float32)
    if cuts:
        values = values * block_levels(rng, shape, cuts, -0.22, 0.18)
    return jnp.clip(values, -most, most).astype(kind)


def setup_inputs(seed: int = 0) -> dict:
    streams_of = jax.random.split(jax.random.key(seed), 9)
    activations = normal_values(streams_of[0], (TOKENS, D), 1.0, 6.0, ((0, 8), (1, 4)))
    cotangent = normal_values(streams_of[1], (TOKENS, D), 1.0, 6.0, ((0, 8), (1, 4)))
    up_tiles = normal_values(streams_of[2], (TILES, BLOCK, BLOCK), (D // 8) ** -0.5, 0.1875, ((0, 16),))
    down_tiles = normal_values(streams_of[3], (TILES, BLOCK, BLOCK), (FF // 8) ** -0.5, 0.125, ((0, 16),))
    up_rows = draw_up_rows(jax.random.fold_in(streams_of[8], 71), 0)
    up_cols = draw_up_cols(jax.random.fold_in(streams_of[8], 71), 0)
    down_rows = draw_down_rows(jax.random.fold_in(streams_of[8], 71), 0)
    down_cols = draw_down_cols(jax.random.fold_in(streams_of[8], 71), 0)
    return {"activations": activations, "cotangent": cotangent, "up_tiles": up_tiles, "down_tiles": down_tiles, "up_rows": up_rows, "up_cols": up_cols, "down_rows": down_rows, "down_cols": down_cols}


inv_root_two = 0.7071067811865476
inv_root_tau = 0.3989422804014327


def gelu_parts(values):
    normal_cdf = 0.5 * (1.0 + jax.scipy.special.erf(values * inv_root_two))
    density = inv_root_tau * jnp.exp(-0.5 * values * values)
    return values * normal_cdf, normal_cdf + values * density


def rank_order(tiles):
    shaped = tiles.reshape(N_FSDP, N_TENSOR, TILE_DEV, BLOCK, BLOCK)
    return shaped.transpose(1, 0, 2, 3, 4).reshape(TILES, BLOCK, BLOCK)


def tile_order(grads):
    shaped = grads.reshape(N_TENSOR, N_FSDP, TILE_DEV, BLOCK, BLOCK)
    return shaped.transpose(1, 0, 2, 3, 4).reshape(TILES, BLOCK, BLOCK)


def apply_tiles(acting, tiles, source, target, segments, letters):
    picked = acting.reshape(TOK_DEV, -1, BLOCK)[:, source].astype(jnp.float32)
    product = jnp.einsum(letters, picked, tiles)
    summed = jnp.zeros((TOK_DEV, segments, BLOCK), jnp.float32).at[:, target].add(product)
    return summed.reshape(TOK_DEV, segments * BLOCK)


def rank_total(partial_value):
    shaped = partial_value.reshape(TOK_DEV, N_TENSOR, D)
    rounded = lax.optimization_barrier(shaped.astype(jnp.bfloat16)).astype(jnp.float32)
    return jnp.sum(rounded, axis=1).astype(jnp.bfloat16)


def outer_tiles(left_side, right_side, left_index, right_index):
    left_pick = left_side.reshape(TOK_DEV, -1, BLOCK)[:, left_index].astype(jnp.float32)
    right_pick = right_side.reshape(TOK_DEV, -1, BLOCK)[:, right_index].astype(jnp.float32)
    term = jnp.einsum("tnb,tnc->nbc", left_pick, right_pick)
    return lax.optimization_barrier(term.astype(jnp.bfloat16)).astype(jnp.float32)


def reference(activations, cotangent, up_tiles, down_tiles, up_rows, up_cols, down_rows, down_cols):
    ranks = jnp.repeat(jnp.arange(N_TENSOR, dtype=jnp.int32), RANK_TILES)
    model_blocks = D // BLOCK
    up_far = up_rows.T.reshape(-1).astype(jnp.int32)
    up_near = ranks * RANK_COLS + up_cols.T.reshape(-1).astype(jnp.int32)
    down_near = ranks * RANK_COLS + down_rows.T.reshape(-1).astype(jnp.int32)
    down_far = down_cols.T.reshape(-1).astype(jnp.int32)
    up_wide = ranks * model_blocks + up_far
    down_wide = ranks * model_blocks + down_far
    up_float = rank_order(up_tiles).astype(jnp.float32)
    down_float = rank_order(down_tiles).astype(jnp.float32)
    groups = TOKENS // TOK_DEV

    def step(carry, blocks_in):
        input_block, cot_block = blocks_in
        pre_act = apply_tiles(input_block, up_float, up_far, up_near, FF // BLOCK, "tnb,nbc->tnc")
        gelu_out, gelu_slope = gelu_parts(pre_act)
        hidden = gelu_out.astype(jnp.bfloat16)
        output = rank_total(apply_tiles(hidden, down_float, down_near, down_wide, N_TENSOR * model_blocks, "tnb,nbc->tnc"))
        hidden_grad = apply_tiles(cot_block, down_float, down_far, down_near, FF // BLOCK, "tnb,ncb->tnc")
        pre_grad = (hidden_grad * gelu_slope).astype(jnp.bfloat16)
        input_grad = rank_total(apply_tiles(pre_grad, up_float, up_near, up_wide, N_TENSOR * model_blocks, "tnb,ncb->tnc"))
        up_term = outer_tiles(input_block, pre_grad, up_far, up_near)
        down_term = outer_tiles(hidden, cot_block, down_near, down_far)
        return (carry[0] + up_term, carry[1] + down_term), (output, input_grad)

    zeros = jnp.zeros((TILES, BLOCK, BLOCK), jnp.float32)
    inputs_split = activations.reshape(groups, TOK_DEV, D)
    cot_split = cotangent.reshape(groups, TOK_DEV, D)
    sums, results = lax.scan(step, (zeros, zeros), (inputs_split, cot_split))
    output = results[0].reshape(TOKENS, D)
    input_grad = results[1].reshape(TOKENS, D)
    return (output, input_grad, tile_order(sums[0]), tile_order(sums[1]))
```

```python
import functools
from itertools import zip_longest

import jax
import jax.numpy as jnp
from jax import lax
from jax.experimental import pallas as pl
from jax.experimental.pallas import tpu as pltpu
from jax.sharding import PartitionSpec as P

MESH = pl.DeviceIdType.MESH
COL_TILES = 8
PIECES = 4

inv_root_two = 0.7071067811865476
inv_root_tau = 0.3989422804014327


def gelu_parts(values):
    normal_cdf = 0.5 * (1.0 + lax.erf(values * inv_root_two))
    density = inv_root_tau * jnp.exp(-0.5 * values * values)
    return (values * normal_cdf, normal_cdf + values * density)


def remote(src, dst, send_sem, recv_sem, where):
    return pltpu.make_async_remote_copy(
        src_ref=src, dst_ref=dst, send_sem=send_sem, recv_sem=recv_sem,
        device_id=where, device_id_type=MESH,
    )


def place(sizes):
    n, chips, replicas = sizes
    z = lax.axis_index("tensor")
    f = lax.axis_index("fsdp")
    y = lax.axis_index("dp")
    return z, f // 2, f % 2, y


def enter(sizes):
    n, chips, replicas = sizes
    z, r, c, y = place(sizes)
    barrier = pltpu.get_barrier_semaphore()

    def greet(where):
        pl.semaphore_signal(barrier, inc=1, device_id=where, device_id_type=MESH)

    @pl.when(z < n - 1)
    def _():
        greet({"tensor": z + 1})

    @pl.when(z > 0)
    def _():
        greet({"tensor": z - 1})

    greet({"fsdp": r * 2 + 1 - c})
    for d in range(1, chips):
        greet({"fsdp": lax.rem(r + d, chips) * 2 + c})
    for e in range(1, replicas):
        greet({"dp": lax.rem(y + e, replicas)})
    sides = jnp.where(z < n - 1, 1, 0) + jnp.where(z > 0, 1, 0)
    pl.semaphore_wait(barrier, sides + 1 + (chips - 1) + (replicas - 1))


def gather_kernel(
    sizes, act, cot, up, down, x_all, c_all, u_all, d_all,
    own_x, own_c, own_u, own_d,
    load_sem, keep_sem, zs_sem, zr_sem, xs_sem, xr_sem, ys_sem, yr_sem, cs_sem, cr_sem,
):
    n, chips, replicas = sizes
    z, r, c, y = place(sizes)
    f = r * 2 + c
    blocks = own_x.shape[0]
    per = up.shape[0]
    part = per // replicas
    features = ((act, own_x, x_all), (cot, own_c, c_all))
    weights = ((up, own_u, u_all), (down, own_d, d_all))

    loads = []
    for a, (src, own, _) in enumerate(features):
        for b in range(blocks):
            copy = pltpu.make_async_copy(
                src.at[:, pl.ds(b * 128, 128)], own.at[b], load_sem.at[a, b]
            )
            copy.start()
            loads.append(copy)
    for a, (src, own, _) in enumerate(weights):
        copy = pltpu.make_async_copy(src, own, load_sem.at[2 + a, 0])
        copy.start()
    enter(sizes)
    for copy in loads:
        copy.wait()

    def shard(full, s):
        return full.at[pl.ds(s * blocks, blocks)]

    def line(a, s, way, source):
        _, own, full = features[a]
        k = 0 if way > 0 else 1
        mine = own if source else shard(full, z - way * s)
        return remote(
            mine, shard(full, z - way * s), zs_sem.at[a, k, s], zr_sem.at[a, k, s],
            {"tensor": z + way},
        )

    def can_send(way):
        return z < n - 1 if way > 0 else z > 0

    def has(s, way):
        return z - s >= 0 if way > 0 else z + s <= n - 1

    for a in range(2):
        for way in (1, -1):

            @pl.when(can_send(way))
            def _():
                line(a, 0, way, True).start()

    def tile_range(full, r_of, c_of, q):
        return full.at[pl.ds((r_of * 2 + c_of) * per + q * part, part)]

    def x_copy(a, d):
        src = weights[a][0].at[pl.ds(y * part, part)]
        return remote(
            src, tile_range(weights[a][2], r, c, y), xs_sem.at[a, d], xr_sem.at[a, d],
            {"fsdp": lax.rem(r + d, chips) * 2 + c},
        )

    for a in range(2):
        for d in range(1, chips):
            x_copy(a, d).start()

    def own_core(a):
        full = weights[a][2]
        return remote(
            weights[a][0], full.at[pl.ds(f * per, per)], cs_sem.at[a, 0, 0], cr_sem.at[a, 0, 0],
            {"fsdp": r * 2 + 1 - c},
        )

    for a in range(2):
        own_core(a).start()

    keeps = []
    for a, (_, own, full) in enumerate(features):
        keeps.append(pltpu.make_async_copy(own, shard(full, z), keep_sem.at[a]))
    for a, (src, own, full) in enumerate(weights):
        pltpu.make_async_copy(src, own, load_sem.at[2 + a, 0]).wait()
        keeps.append(
            pltpu.make_async_copy(own, full.at[pl.ds(f * per, per)], keep_sem.at[2 + a])
        )
    for copy in keeps:
        copy.start()

    def y_copy(a, d, e):
        piece = tile_range(weights[a][2], lax.rem(r - d + chips, chips), c, y)
        return remote(
            piece, piece, ys_sem.at[a, d, e], yr_sem.at[a, d, e],
            {"dp": lax.rem(y + e, replicas)},
        )

    def core_copy(a, d, e):
        q = lax.rem(y - e + replicas, replicas)
        piece = tile_range(weights[a][2], lax.rem(r - d + chips, chips), c, q)
        return remote(
            piece, piece, cs_sem.at[a, d, e], cr_sem.at[a, d, e], {"fsdp": r * 2 + 1 - c}
        )

    def z_event(s):
        for a in range(2):
            for way in (1, -1):

                @pl.when(has(s, way))
                def _():
                    line(a, s - 1, way, False).wait_recv()

                    if s < n - 1:

                        @pl.when(can_send(way))
                        def _():
                            line(a, s, way, False).start()

    def x_event(a):
        for d in range(1, chips):
            x_copy(a, d).wait_recv()
            for e in range(1, replicas):
                y_copy(a, d, e).start()
            core_copy(a, d, 0).start()

    def y_event(a):
        for d in range(1, chips):
            for e in range(1, replicas):
                y_copy(a, d, e).wait_recv()
                core_copy(a, d, e).start()

    tile_events = [
        lambda: x_event(0),
        lambda: (x_event(1), y_event(0)),
        lambda: y_event(1),
    ]
    z_events = [functools.partial(z_event, s) for s in range(1, n)]
    for first, second in zip_longest(z_events, tile_events):
        if first is not None:
            first()
        if second is not None:
            second()

    for copy in keeps:
        copy.wait()
    for a in range(2):
        own_core(a).wait()
        for d in range(1, chips):
            x_copy(a, d).wait_send()
            core_copy(a, d, 0).wait()
            for e in range(1, replicas):
                y_copy(a, d, e).wait_send()
                core_copy(a, d, e).wait()
        for way in (1, -1):
            for s in range(n - 1):

                @pl.when(jnp.logical_and(can_send(way), has(s, way)))
                def _():
                    line(a, s, way, s == 0).wait_send()


def gather(sizes, activations, cotangent, up_tiles, down_tiles):
    n, chips, replicas = sizes
    rows, wide = activations.shape
    blocks = wide // 128
    per = up_tiles.shape[0]
    kind = jnp.bfloat16
    dma = pltpu.SemaphoreType.DMA
    anywhere = pl.BlockSpec(memory_space=pl.ANY)
    return pl.pallas_call(
        functools.partial(gather_kernel, sizes),
        out_shape=(
            jax.ShapeDtypeStruct((n * blocks, rows, 128), kind),
            jax.ShapeDtypeStruct((n * blocks, rows, 128), kind),
            jax.ShapeDtypeStruct((2 * chips * per, 128, 128), kind),
            jax.ShapeDtypeStruct((2 * chips * per, 128, 128), kind),
        ),
        in_specs=[anywhere] * 4,
        out_specs=(anywhere,) * 4,
        scratch_shapes=[
            pltpu.VMEM((blocks, rows, 128), kind),
            pltpu.VMEM((blocks, rows, 128), kind),
            pltpu.VMEM((per, 128, 128), kind),
            pltpu.VMEM((per, 128, 128), kind),
            dma((4, blocks)),
            dma((4,)),
            dma((2, 2, n)),
            dma((2, 2, n)),
            dma((2, chips)),
            dma((2, chips)),
            dma((2, chips, replicas)),
            dma((2, chips, replicas)),
            dma((2, chips, replicas)),
            dma((2, chips, replicas)),
        ],
        compiler_params=pltpu.CompilerParams(collective_id=0, has_side_effects=True),
        name="gather_all",
    )(activations, cotangent, up_tiles, down_tiles)


def mm(a, b, ca, cb):
    return lax.dot_general(a, b, (((ca,), (cb,)), ((), ())), preferred_element_type=jnp.float32)


def local_kernel(
    hidden_blocks, uo, uf, do, df, x, c, u, d, out, inp, ug, dg, xt, out_acc, inp_acc
):
    model_blocks = x.shape[0]

    @pl.loop(0, model_blocks)
    def _(b):
        xt[b] = x[b].T
        out_acc[b] = jnp.zeros_like(out_acc[b])
        inp_acc[b] = jnp.zeros_like(inp_acc[b])

    @pl.loop(0, hidden_blocks)
    def _(h):
        first = h * COL_TILES
        ui = [uo[first + k] for k in range(COL_TILES)]
        uj = [uf[first + k] for k in range(COL_TILES)]
        di = [do[first + k] for k in range(COL_TILES)]
        dj = [df[first + k] for k in range(COL_TILES)]
        pre = mm(x[uj[0]], u[ui[0]], 1, 0)
        hidden_grad = mm(c[dj[0]], d[di[0]], 1, 1)
        for k in range(1, COL_TILES):
            pre += mm(x[uj[k]], u[ui[k]], 1, 0)
            hidden_grad += mm(c[dj[k]], d[di[k]], 1, 1)
        value, slope = gelu_parts(pre)
        hidden = value.astype(jnp.bfloat16)
        pre_grad = (hidden_grad * slope).astype(jnp.bfloat16)
        hidden_t = hidden.T
        for k in range(COL_TILES):
            out_acc[dj[k]] += mm(hidden, d[di[k]], 1, 0)
            inp_acc[uj[k]] += mm(pre_grad, u[ui[k]], 1, 1)
            ug[ui[k]] = mm(xt[uj[k]], pre_grad, 1, 0).astype(jnp.bfloat16)
            dg[di[k]] = mm(hidden_t, c[dj[k]], 1, 0).astype(jnp.bfloat16)

    @pl.loop(0, model_blocks)
    def _(b):
        out[b] = out_acc[b].astype(jnp.bfloat16)
        inp[b] = inp_acc[b].astype(jnp.bfloat16)


def local(tables, x, c, u, d):
    vmem = pl.BlockSpec(memory_space=pltpu.VMEM)
    smem = pl.BlockSpec(memory_space=pltpu.SMEM)
    hidden_blocks = u.shape[0] // COL_TILES
    return pl.pallas_call(
        functools.partial(local_kernel, hidden_blocks),
        out_shape=tuple(jax.ShapeDtypeStruct(v.shape, jnp.bfloat16) for v in (x, x, u, u)),
        in_specs=[smem] * 4 + [vmem] * 4,
        out_specs=(vmem,) * 4,
        scratch_shapes=[
            pltpu.VMEM((x.shape[0], 128, x.shape[1]), jnp.bfloat16),
            pltpu.VMEM(x.shape, jnp.float32),
            pltpu.VMEM(x.shape, jnp.float32),
        ],
        compiler_params=pltpu.CompilerParams(vmem_limit_bytes=60 * 1024 * 1024),
        name="local_work",
    )(*tables, x, c, u, d)


def add_into(target, terms):
    @pl.loop(0, target.shape[0])
    def _(b):
        total = terms[0][b].astype(jnp.float32)
        for term in terms[1:]:
            total += term[b].astype(jnp.float32)
        target[b] = total.astype(target.dtype)


def reduce_kernel(
    sizes, out_part, inp_part, ug, dg, out, inp, ga_u, ga_d, gb_u, gb_d,
    held_r, held_l, own, core_in, x_in,
    own_sem, zs_sem, zr_sem, cs_sem, cr_sem, xs_sem, xr_sem, ys_sem, yr_sem,
):
    n, chips, replicas = sizes
    z, r, c, y = place(sizes)
    blocks = out.shape[0]
    per = ga_u.shape[0]
    size = per // PIECES
    parts = (out_part, inp_part)
    outs = (out, inp)
    grads = (ug, dg)
    sums = (ga_u, ga_d)
    others = (gb_u, gb_d)
    held = (held_r, held_l)

    def tiles(ref, r_of, c_of, k):
        return ref.at[pl.ds((r_of * 2 + c_of) * per + k * size, size)]

    def own_copy(a, k, q):
        return pltpu.make_async_copy(
            tiles(grads[a], q, c, k), own.at[a, q, pl.ds(k * size, size)], own_sem.at[a, k, q]
        )

    for a in range(2):
        for k in range(PIECES):
            for q in range(chips):
                own_copy(a, k, q).start()
    enter(sizes)

    def core_copy(a, k, q):
        return remote(
            tiles(grads[a], q, 1 - c, k), core_in.at[a, q, pl.ds(k * size, size)],
            cs_sem.at[a, k, q], cr_sem.at[a, k, q], {"fsdp": r * 2 + 1 - c},
        )

    def shard(ref, s):
        return ref.at[pl.ds(s * blocks, blocks)]

    def line(a, i, way, source):
        s = n - 1 - i if way > 0 else i
        k = 0 if way > 0 else 1
        src = shard(parts[a], s) if source else held[k].at[a, i]
        return remote(
            src, held[k].at[a, i], zs_sem.at[a, k, i], zr_sem.at[a, k, i], {"tensor": z + way}
        )

    def edge(way):
        return z == 0 if way > 0 else z == n - 1

    def sends(i, way):
        return n - 1 - i > z if way > 0 else i < z

    def keeps(i, way):
        return n - 1 - i == z if way > 0 else i == z

    def z_start():
        for i in range(n - 1):
            for a in range(2):
                for way in (1, -1):

                    @pl.when(edge(way))
                    def _():
                        line(a, i, way, True).start()

    def z_event(i, a):
        for way in (1, -1):
            s = n - 1 - i if way > 0 else i
            k = 0 if way > 0 else 1

            @pl.when(jnp.logical_and(sends(i, way), jnp.logical_not(edge(way))))
            def _():
                line(a, i, way, False).wait_recv()
                add_into(held[k].at[a, i], (held[k].at[a, i], shard(parts[a], s)))
                line(a, i, way, False).start()

    for a in range(2):
        for k in range(PIECES):
            for q in range(chips):
                core_copy(a, k, q).start()
        if a == 0:
            z_start()

    def x_copy(a, k, d):
        q = lax.rem(r + d, chips)
        return remote(
            core_in.at[a, q, pl.ds(k * size, size)], x_in.at[a, d, pl.ds(k * size, size)],
            xs_sem.at[a, k, d], xr_sem.at[a, k, d], {"fsdp": q * 2 + c},
        )

    def y_copy(a, k, e):
        return remote(
            sums[a].at[pl.ds(k * size, size)], others[a].at[e - 1, pl.ds(k * size, size)],
            ys_sem.at[a, k, e], yr_sem.at[a, k, e], {"dp": lax.rem(y + e, replicas)},
        )

    for a in range(2):
        for k in range(PIECES):
            for d in range(1, chips):
                q = lax.rem(r + d, chips)
                own_copy(a, k, q).wait()
                core_copy(a, k, q).wait_recv()
                mine = core_in.at[a, q, pl.ds(k * size, size)]
                add_into(mine, (mine, own.at[a, q, pl.ds(k * size, size)]))
                x_copy(a, k, d).start()

    def x_event(a, k):
        here = pl.ds(k * size, size)
        own_copy(a, k, r).wait()
        core_copy(a, k, r).wait_recv()
        for d in range(1, chips):
            x_copy(a, k, d).wait_recv()
        add_into(
            sums[a].at[here],
            [own.at[a, r, here], core_in.at[a, r, here]]
            + [x_in.at[a, d, here] for d in range(1, chips)],
        )
        for e in range(1, replicas):
            y_copy(a, k, e).start()

    z_events = [functools.partial(z_event, i, a) for i in range(n - 1) for a in range(2)]
    x_events = [functools.partial(x_event, a, k) for a in range(2) for k in range(PIECES)]
    for first, second in zip_longest(z_events, x_events):
        if first is not None:
            first()
        if second is not None:
            second()

    for a in range(2):
        mine = shard(parts[a], z)

        @pl.when(z > 0)
        def _():
            line(a, n - 1 - z, 1, False).wait_recv()

        @pl.when(z < n - 1)
        def _():
            line(a, z, -1, False).wait_recv()

        @pl.when(z == 0)
        def _():
            add_into(outs[a], (mine, held_l.at[a, z]))

        @pl.when(z == n - 1)
        def _():
            add_into(outs[a], (mine, held_r.at[a, n - 1 - z]))

        @pl.when(jnp.logical_and(z > 0, z < n - 1))
        def _():
            add_into(outs[a], (mine, held_r.at[a, n - 1 - z], held_l.at[a, z]))

        for i in range(n - 1):
            for way in (1, -1):

                @pl.when(sends(i, way))
                def _():
                    line(a, i, way, False).wait_send()

        for k in range(PIECES):
            for q in range(chips):
                core_copy(a, k, q).wait_send()
            for d in range(1, chips):
                x_copy(a, k, d).wait_send()
            for e in range(1, replicas):
                y_copy(a, k, e).wait()


def reduce(sizes, out_part, inp_part, ug, dg):
    n, chips, replicas = sizes
    blocks = out_part.shape[0] // n
    rows = out_part.shape[1]
    per = ug.shape[0] // (2 * chips)
    kind = jnp.bfloat16
    dma = pltpu.SemaphoreType.DMA
    vmem = pl.BlockSpec(memory_space=pltpu.VMEM)
    anywhere = pl.BlockSpec(memory_space=pl.ANY)
    return pl.pallas_call(
        functools.partial(reduce_kernel, sizes),
        out_shape=(
            [jax.ShapeDtypeStruct((blocks, rows, 128), kind)] * 2
            + [jax.ShapeDtypeStruct((per, 128, 128), kind)] * 2
            + [jax.ShapeDtypeStruct((replicas - 1, per, 128, 128), kind)] * 2
        ),
        in_specs=[vmem, vmem, anywhere, anywhere],
        out_specs=[vmem] * 4 + [anywhere] * 2,
        scratch_shapes=[
            pltpu.VMEM((2, n, blocks, rows, 128), kind),
            pltpu.VMEM((2, n, blocks, rows, 128), kind),
            pltpu.VMEM((2, chips, per, 128, 128), kind),
            pltpu.VMEM((2, chips, per, 128, 128), kind),
            pltpu.VMEM((2, chips, per, 128, 128), kind),
            dma((2, PIECES, chips)),
            dma((2, 2, n)),
            dma((2, 2, n)),
            dma((2, PIECES, chips)),
            dma((2, PIECES, chips)),
            dma((2, PIECES, chips)),
            dma((2, PIECES, chips)),
            dma((2, PIECES, replicas)),
            dma((2, PIECES, replicas)),
        ],
        compiler_params=pltpu.CompilerParams(
            collective_id=1, has_side_effects=True, vmem_limit_bytes=60 * 1024 * 1024
        ),
        name="reduce_all",
    )(out_part, inp_part, ug, dg)


def tables_of(near, far):
    count = near.shape[0]
    at = lax.iota(jnp.int32, count)
    earlier = (near[:, None] == near[None, :]) & (at[:, None] < at[None, :])
    spot = near * COL_TILES + jnp.sum(earlier.astype(jnp.int32), axis=0)
    here = spot[:, None] == at[None, :]
    order = jnp.sum(jnp.where(here, at[:, None], 0), axis=0)
    far_order = jnp.sum(jnp.where(here, far[:, None], 0), axis=0)
    return order, far_order


def body(sizes, activations, cotangent, up_tiles, down_tiles, up_rows, up_cols, down_rows, down_cols):
    up_order, up_far = tables_of(up_cols[:, 0], up_rows[:, 0])
    down_order, down_far = tables_of(down_rows[:, 0], down_cols[:, 0])
    full = gather(sizes, activations, cotangent, up_tiles, down_tiles)
    parts = local((up_order, up_far, down_order, down_far), *full)
    out, inp, ga_u, ga_d, gb_u, gb_d = reduce(sizes, *parts)

    def flat(v):
        return v.transpose(1, 0, 2).reshape(v.shape[1], -1)

    def total(a, b):
        return a.astype(jnp.float32) + jnp.sum(b.astype(jnp.float32), axis=0)

    return flat(out), flat(inp), total(ga_u, gb_u), total(ga_d, gb_d)


def solution(mesh):
    sizes = (mesh.shape["tensor"], mesh.shape["fsdp"] // 2, mesh.shape["dp"])
    in_specs = (
        P(("dp", "fsdp"), "tensor"),
        P(("dp", "fsdp"), "tensor"),
        P(("fsdp", "tensor"), None, None),
        P(("fsdp", "tensor"), None, None),
        P(None, "tensor"),
        P(None, "tensor"),
        P(None, "tensor"),
        P(None, "tensor"),
    )
    out_specs = (
        P(("dp", "fsdp"), "tensor"),
        P(("dp", "fsdp"), "tensor"),
        P(("fsdp", "tensor"), None, None),
        P(("fsdp", "tensor"), None, None),
    )
    return jax.shard_map(
        functools.partial(body, sizes), mesh=mesh, in_specs=in_specs, out_specs=out_specs,
        check_vma=False,
    )
```

```python
import functools
from itertools import zip_longest

import jax
import jax.numpy as jnp
from jax import lax
from jax.experimental import pallas as pl
from jax.experimental.pallas import tpu as pltpu
from jax.sharding import PartitionSpec as P

MESH = pl.DeviceIdType.MESH
COL_TILES = 8
PIECES = 8
AHEAD = 4

inv_root_two = 0.7071067811865476
inv_root_tau = 0.3989422804014327


def gelu_parts(values):
    normal_cdf = 0.5 * (1.0 + lax.erf(values * inv_root_two))
    density = inv_root_tau * jnp.exp(-0.5 * values * values)
    return (values * normal_cdf, normal_cdf + values * density)


def remote(src, dst, send_sem, recv_sem, where):
    return pltpu.make_async_remote_copy(
        src_ref=src, dst_ref=dst, send_sem=send_sem, recv_sem=recv_sem,
        device_id=where, device_id_type=MESH,
    )


def place(sizes):
    n, chips, replicas = sizes
    z = lax.axis_index("tensor")
    f = lax.axis_index("fsdp")
    y = lax.axis_index("dp")
    return z, f // 2, f % 2, y


def enter(sizes):
    n, chips, replicas = sizes
    z, r, c, y = place(sizes)
    barrier = pltpu.get_barrier_semaphore()

    def greet(where):
        pl.semaphore_signal(barrier, inc=1, device_id=where, device_id_type=MESH)

    @pl.when(z < n - 1)
    def _():
        greet({"tensor": z + 1})

    @pl.when(z > 0)
    def _():
        greet({"tensor": z - 1})

    greet({"fsdp": r * 2 + 1 - c})
    for d in range(1, chips):
        greet({"fsdp": lax.rem(r + d, chips) * 2 + c})
    for e in range(1, replicas):
        greet({"dp": lax.rem(y + e, replicas)})
    sides = jnp.where(z < n - 1, 1, 0) + jnp.where(z > 0, 1, 0)
    pl.semaphore_wait(barrier, sides + 1 + (chips - 1) + (replicas - 1))


def gather_kernel(
    sizes, act, cot, up, down, x_all, c_all, u_all, d_all,
    own_x, own_c, own_u, own_d,
    load_sem, keep_sem, zs_sem, zr_sem, xs_sem, xr_sem, ys_sem, yr_sem, cs_sem, cr_sem,
):
    n, chips, replicas = sizes
    z, r, c, y = place(sizes)
    f = r * 2 + c
    blocks = own_x.shape[0]
    per = up.shape[0]
    part = per // replicas
    features = ((act, own_x, x_all), (cot, own_c, c_all))
    weights = ((up, own_u, u_all), (down, own_d, d_all))

    loads = []
    for a, (src, own, _) in enumerate(features):
        for b in range(blocks):
            copy = pltpu.make_async_copy(
                src.at[:, pl.ds(b * 128, 128)], own.at[b], load_sem.at[a, b]
            )
            copy.start()
            loads.append(copy)
    for a, (src, own, _) in enumerate(weights):
        copy = pltpu.make_async_copy(src, own, load_sem.at[2 + a, 0])
        copy.start()
    enter(sizes)
    for copy in loads:
        copy.wait()

    def shard(full, s):
        return full.at[pl.ds(s * blocks, blocks)]

    def line(a, s, way, source):
        _, own, full = features[a]
        k = 0 if way > 0 else 1
        mine = own if source else shard(full, z - way * s)
        return remote(
            mine, shard(full, z - way * s), zs_sem.at[a, k, s], zr_sem.at[a, k, s],
            {"tensor": z + way},
        )

    def can_send(way):
        return z < n - 1 if way > 0 else z > 0

    def has(s, way):
        return z - s >= 0 if way > 0 else z + s <= n - 1

    for a in range(2):
        for way in (1, -1):

            @pl.when(can_send(way))
            def _():
                line(a, 0, way, True).start()

    def tile_range(full, r_of, c_of, q):
        return full.at[pl.ds((r_of * 2 + c_of) * per + q * part, part)]

    def x_copy(a, d):
        src = weights[a][0].at[pl.ds(y * part, part)]
        return remote(
            src, tile_range(weights[a][2], r, c, y), xs_sem.at[a, d], xr_sem.at[a, d],
            {"fsdp": lax.rem(r + d, chips) * 2 + c},
        )

    for a in range(2):
        for d in range(1, chips):
            x_copy(a, d).start()

    def own_core(a):
        full = weights[a][2]
        return remote(
            weights[a][0], full.at[pl.ds(f * per, per)], cs_sem.at[a, 0, 0], cr_sem.at[a, 0, 0],
            {"fsdp": r * 2 + 1 - c},
        )

    for a in range(2):
        own_core(a).start()

    keeps = []
    for a, (_, own, full) in enumerate(features):
        keeps.append(pltpu.make_async_copy(own, shard(full, z), keep_sem.at[a]))
    for a, (src, own, full) in enumerate(weights):
        pltpu.make_async_copy(src, own, load_sem.at[2 + a, 0]).wait()
        keeps.append(
            pltpu.make_async_copy(own, full.at[pl.ds(f * per, per)], keep_sem.at[2 + a])
        )
    for copy in keeps:
        copy.start()

    def y_copy(a, d, e):
        piece = tile_range(weights[a][2], lax.rem(r - d + chips, chips), c, y)
        return remote(
            piece, piece, ys_sem.at[a, d, e], yr_sem.at[a, d, e],
            {"dp": lax.rem(y + e, replicas)},
        )

    def core_copy(a, d, e):
        q = lax.rem(y - e + replicas, replicas)
        piece = tile_range(weights[a][2], lax.rem(r - d + chips, chips), c, q)
        return remote(
            piece, piece, cs_sem.at[a, d, e], cr_sem.at[a, d, e], {"fsdp": r * 2 + 1 - c}
        )

    def z_event(s):
        for a in range(2):
            for way in (1, -1):

                @pl.when(has(s, way))
                def _():
                    line(a, s - 1, way, False).wait_recv()

                    if s < n - 1:

                        @pl.when(can_send(way))
                        def _():
                            line(a, s, way, False).start()

    def x_event(a):
        for d in range(1, chips):
            x_copy(a, d).wait_recv()
            for e in range(1, replicas):
                y_copy(a, d, e).start()
            core_copy(a, d, 0).start()

    def y_event(a):
        for d in range(1, chips):
            for e in range(1, replicas):
                y_copy(a, d, e).wait_recv()
                core_copy(a, d, e).start()

    tile_events = [
        lambda: x_event(0),
        lambda: (x_event(1), y_event(0)),
        lambda: y_event(1),
    ]
    z_events = [functools.partial(z_event, s) for s in range(1, n)]
    for first, second in zip_longest(z_events, tile_events):
        if first is not None:
            first()
        if second is not None:
            second()

    for copy in keeps:
        copy.wait()
    for a in range(2):
        own_core(a).wait()
        for d in range(1, chips):
            x_copy(a, d).wait_send()
            core_copy(a, d, 0).wait()
            for e in range(1, replicas):
                y_copy(a, d, e).wait_send()
                core_copy(a, d, e).wait()
        for way in (1, -1):
            for s in range(n - 1):

                @pl.when(jnp.logical_and(can_send(way), has(s, way)))
                def _():
                    line(a, s, way, s == 0).wait_send()


def gather(sizes, activations, cotangent, up_tiles, down_tiles):
    n, chips, replicas = sizes
    rows, wide = activations.shape
    blocks = wide // 128
    per = up_tiles.shape[0]
    kind = jnp.bfloat16
    dma = pltpu.SemaphoreType.DMA
    anywhere = pl.BlockSpec(memory_space=pl.ANY)
    return pl.pallas_call(
        functools.partial(gather_kernel, sizes),
        out_shape=(
            jax.ShapeDtypeStruct((n * blocks, rows, 128), kind),
            jax.ShapeDtypeStruct((n * blocks, rows, 128), kind),
            jax.ShapeDtypeStruct((2 * chips * per, 128, 128), kind),
            jax.ShapeDtypeStruct((2 * chips * per, 128, 128), kind),
        ),
        in_specs=[anywhere] * 4,
        out_specs=(anywhere,) * 4,
        scratch_shapes=[
            pltpu.VMEM((blocks, rows, 128), kind),
            pltpu.VMEM((blocks, rows, 128), kind),
            pltpu.VMEM((per, 128, 128), kind),
            pltpu.VMEM((per, 128, 128), kind),
            dma((4, blocks)),
            dma((4,)),
            dma((2, 2, n)),
            dma((2, 2, n)),
            dma((2, chips)),
            dma((2, chips)),
            dma((2, chips, replicas)),
            dma((2, chips, replicas)),
            dma((2, chips, replicas)),
            dma((2, chips, replicas)),
        ],
        compiler_params=pltpu.CompilerParams(collective_id=0, has_side_effects=True),
        name="gather_all",
    )(activations, cotangent, up_tiles, down_tiles)


def mm(a, b, ca, cb):
    return lax.dot_general(a, b, (((ca,), (cb,)), ((), ())), preferred_element_type=jnp.float32)


def local_kernel(
    hidden_blocks, uo, uf, do, df, x, c, u, d, out, inp, ug, dg, xt, out_acc, inp_acc
):
    model_blocks = x.shape[0]

    @pl.loop(0, model_blocks)
    def _(b):
        xt[b] = x[b].T
        out_acc[b] = jnp.zeros_like(out_acc[b])
        inp_acc[b] = jnp.zeros_like(inp_acc[b])

    @pl.loop(0, hidden_blocks)
    def _(h):
        first = h * COL_TILES
        ui = [uo[first + k] for k in range(COL_TILES)]
        uj = [uf[first + k] for k in range(COL_TILES)]
        di = [do[first + k] for k in range(COL_TILES)]
        dj = [df[first + k] for k in range(COL_TILES)]
        pre = mm(x[uj[0]], u[ui[0]], 1, 0)
        hidden_grad = mm(c[dj[0]], d[di[0]], 1, 1)
        for k in range(1, COL_TILES):
            pre += mm(x[uj[k]], u[ui[k]], 1, 0)
            hidden_grad += mm(c[dj[k]], d[di[k]], 1, 1)
        value, slope = gelu_parts(pre)
        hidden = value.astype(jnp.bfloat16)
        pre_grad = (hidden_grad * slope).astype(jnp.bfloat16)
        hidden_t = hidden.T
        for k in range(COL_TILES):
            out_acc[dj[k]] += mm(hidden, d[di[k]], 1, 0)
            inp_acc[uj[k]] += mm(pre_grad, u[ui[k]], 1, 1)
            ug[ui[k]] = mm(xt[uj[k]], pre_grad, 1, 0).astype(jnp.bfloat16)
            dg[di[k]] = mm(hidden_t, c[dj[k]], 1, 0).astype(jnp.bfloat16)

    @pl.loop(0, model_blocks)
    def _(b):
        out[b] = out_acc[b].astype(jnp.bfloat16)
        inp[b] = inp_acc[b].astype(jnp.bfloat16)


def local(tables, x, c, u, d):
    vmem = pl.BlockSpec(memory_space=pltpu.VMEM)
    smem = pl.BlockSpec(memory_space=pltpu.SMEM)
    hidden_blocks = u.shape[0] // COL_TILES
    return pl.pallas_call(
        functools.partial(local_kernel, hidden_blocks),
        out_shape=tuple(jax.ShapeDtypeStruct(v.shape, jnp.bfloat16) for v in (x, x, u, u)),
        in_specs=[smem] * 4 + [vmem] * 4,
        out_specs=(vmem,) * 4,
        scratch_shapes=[
            pltpu.VMEM((x.shape[0], 128, x.shape[1]), jnp.bfloat16),
            pltpu.VMEM(x.shape, jnp.float32),
            pltpu.VMEM(x.shape, jnp.float32),
        ],
        compiler_params=pltpu.CompilerParams(vmem_limit_bytes=60 * 1024 * 1024),
        name="local_work",
    )(*tables, x, c, u, d)


def add_into(target, terms):
    @pl.loop(0, target.shape[0])
    def _(b):
        total = terms[0][b].astype(jnp.float32)
        for term in terms[1:]:
            total += term[b].astype(jnp.float32)
        target[b] = total.astype(target.dtype)


def reduce_kernel(
    sizes, out_part, inp_part, ug, dg, out, inp, ga_u, ga_d, gb_u, gb_d,
    held_r, held_l, own, core_in, x_in,
    own_sem, zs_sem, zr_sem, cs_sem, cr_sem, xs_sem, xr_sem, ys_sem, yr_sem,
):
    n, chips, replicas = sizes
    z, r, c, y = place(sizes)
    blocks = out.shape[0]
    per = ga_u.shape[0]
    size = per // PIECES
    parts = (out_part, inp_part)
    outs = (out, inp)
    grads = (ug, dg)
    sums = (ga_u, ga_d)
    others = (gb_u, gb_d)
    held = (held_r, held_l)

    def tiles(ref, r_of, c_of, k):
        return ref.at[pl.ds((r_of * 2 + c_of) * per + k * size, size)]

    def own_copy(a, k, q):
        return pltpu.make_async_copy(
            tiles(grads[a], q, c, k), own.at[a, q, pl.ds(k * size, size)], own_sem.at[a, k, q]
        )

    for a in range(2):
        for k in range(PIECES):
            for q in range(chips):
                own_copy(a, k, q).start()
    enter(sizes)

    def core_copy(a, k, q):
        return remote(
            tiles(grads[a], q, 1 - c, k), core_in.at[a, q, pl.ds(k * size, size)],
            cs_sem.at[a, k, q], cr_sem.at[a, k, q], {"fsdp": r * 2 + 1 - c},
        )

    def shard(ref, s):
        return ref.at[pl.ds(s * blocks, blocks)]

    def line(a, i, way, source):
        s = n - 1 - i if way > 0 else i
        k = 0 if way > 0 else 1
        src = shard(parts[a], s) if source else held[k].at[a, i]
        return remote(
            src, held[k].at[a, i], zs_sem.at[a, k, i], zr_sem.at[a, k, i], {"tensor": z + way}
        )

    def edge(way):
        return z == 0 if way > 0 else z == n - 1

    def sends(i, way):
        return n - 1 - i > z if way > 0 else i < z

    def keeps(i, way):
        return n - 1 - i == z if way > 0 else i == z

    def z_start():
        for i in range(n - 1):
            for a in range(2):
                for way in (1, -1):

                    @pl.when(edge(way))
                    def _():
                        line(a, i, way, True).start()

    def z_event(t, a):
        for way in (1, -1):
            i = t - z if way > 0 else t - (n - 1 - z)
            s = n - 1 - i if way > 0 else i
            k = 0 if way > 0 else 1
            on_way = jnp.logical_and(i >= 0, sends(i, way))

            @pl.when(jnp.logical_and(on_way, jnp.logical_not(edge(way))))
            def _():
                line(a, i, way, False).wait_recv()
                add_into(held[k].at[a, i], (held[k].at[a, i], shard(parts[a], s)))
                line(a, i, way, False).start()

    for a in range(2):
        for k in range(PIECES):
            for q in range(chips):
                core_copy(a, k, q).start()
        if a == 0:
            z_start()

    def x_copy(a, k, d):
        q = lax.rem(r + d, chips)
        return remote(
            core_in.at[a, q, pl.ds(k * size, size)], x_in.at[a, d, pl.ds(k * size, size)],
            xs_sem.at[a, k, d], xr_sem.at[a, k, d], {"fsdp": q * 2 + c},
        )

    def y_copy(a, k, e):
        return remote(
            sums[a].at[pl.ds(k * size, size)], others[a].at[e - 1, pl.ds(k * size, size)],
            ys_sem.at[a, k, e], yr_sem.at[a, k, e], {"dp": lax.rem(y + e, replicas)},
        )

    def feed(a, k):
        for d in range(1, chips):
            q = lax.rem(r + d, chips)
            own_copy(a, k, q).wait()
            core_copy(a, k, q).wait_recv()
            mine = core_in.at[a, q, pl.ds(k * size, size)]
            add_into(mine, (mine, own.at[a, q, pl.ds(k * size, size)]))
            x_copy(a, k, d).start()

    def x_event(a, k):
        here = pl.ds(k * size, size)
        own_copy(a, k, r).wait()
        core_copy(a, k, r).wait_recv()
        for d in range(1, chips):
            x_copy(a, k, d).wait_recv()
        add_into(
            sums[a].at[here],
            [own.at[a, r, here], core_in.at[a, r, here]]
            + [x_in.at[a, d, here] for d in range(1, chips)],
        )
        for e in range(1, replicas):
            y_copy(a, k, e).start()

    pieces = [(a, k) for a in range(2) for k in range(PIECES)]
    slots = [(t, a) for t in range(1, n - 1) for a in range(2)]
    for piece in pieces[:AHEAD]:
        feed(*piece)
    for i, piece in enumerate(pieces):
        if i % 2 == 0 and i >= 2 and slots:
            z_event(*slots.pop(0))
        if i + AHEAD < len(pieces):
            feed(*pieces[i + AHEAD])
        x_event(*piece)
    for slot in slots:
        z_event(*slot)

    for a in range(2):
        mine = shard(parts[a], z)

        @pl.when(z > 0)
        def _():
            line(a, n - 1 - z, 1, False).wait_recv()

        @pl.when(z < n - 1)
        def _():
            line(a, z, -1, False).wait_recv()

        @pl.when(z == 0)
        def _():
            add_into(outs[a], (mine, held_l.at[a, z]))

        @pl.when(z == n - 1)
        def _():
            add_into(outs[a], (mine, held_r.at[a, n - 1 - z]))

        @pl.when(jnp.logical_and(z > 0, z < n - 1))
        def _():
            add_into(outs[a], (mine, held_r.at[a, n - 1 - z], held_l.at[a, z]))

        for i in range(n - 1):
            for way in (1, -1):

                @pl.when(sends(i, way))
                def _():
                    line(a, i, way, False).wait_send()

        for k in range(PIECES):
            for q in range(chips):
                core_copy(a, k, q).wait_send()
            for d in range(1, chips):
                x_copy(a, k, d).wait_send()
            for e in range(1, replicas):
                y_copy(a, k, e).wait()


def reduce(sizes, out_part, inp_part, ug, dg):
    n, chips, replicas = sizes
    blocks = out_part.shape[0] // n
    rows = out_part.shape[1]
    per = ug.shape[0] // (2 * chips)
    kind = jnp.bfloat16
    dma = pltpu.SemaphoreType.DMA
    vmem = pl.BlockSpec(memory_space=pltpu.VMEM)
    anywhere = pl.BlockSpec(memory_space=pl.ANY)
    return pl.pallas_call(
        functools.partial(reduce_kernel, sizes),
        out_shape=(
            [jax.ShapeDtypeStruct((blocks, rows, 128), kind)] * 2
            + [jax.ShapeDtypeStruct((per, 128, 128), kind)] * 2
            + [jax.ShapeDtypeStruct((replicas - 1, per, 128, 128), kind)] * 2
        ),
        in_specs=[vmem, vmem, anywhere, anywhere],
        out_specs=[vmem] * 4 + [anywhere] * 2,
        scratch_shapes=[
            pltpu.VMEM((2, n, blocks, rows, 128), kind),
            pltpu.VMEM((2, n, blocks, rows, 128), kind),
            pltpu.VMEM((2, chips, per, 128, 128), kind),
            pltpu.VMEM((2, chips, per, 128, 128), kind),
            pltpu.VMEM((2, chips, per, 128, 128), kind),
            dma((2, PIECES, chips)),
            dma((2, 2, n)),
            dma((2, 2, n)),
            dma((2, PIECES, chips)),
            dma((2, PIECES, chips)),
            dma((2, PIECES, chips)),
            dma((2, PIECES, chips)),
            dma((2, PIECES, replicas)),
            dma((2, PIECES, replicas)),
        ],
        compiler_params=pltpu.CompilerParams(
            collective_id=1, has_side_effects=True, vmem_limit_bytes=60 * 1024 * 1024
        ),
        name="reduce_all",
    )(out_part, inp_part, ug, dg)


def tables_of(near, far):
    count = near.shape[0]
    at = lax.iota(jnp.int32, count)
    earlier = (near[:, None] == near[None, :]) & (at[:, None] < at[None, :])
    spot = near * COL_TILES + jnp.sum(earlier.astype(jnp.int32), axis=0)
    here = spot[:, None] == at[None, :]
    order = jnp.sum(jnp.where(here, at[:, None], 0), axis=0)
    far_order = jnp.sum(jnp.where(here, far[:, None], 0), axis=0)
    return order, far_order


def body(sizes, activations, cotangent, up_tiles, down_tiles, up_rows, up_cols, down_rows, down_cols):
    up_order, up_far = tables_of(up_cols[:, 0], up_rows[:, 0])
    down_order, down_far = tables_of(down_rows[:, 0], down_cols[:, 0])
    full = gather(sizes, activations, cotangent, up_tiles, down_tiles)
    parts = local((up_order, up_far, down_order, down_far), *full)
    out, inp, ga_u, ga_d, gb_u, gb_d = reduce(sizes, *parts)

    def flat(v):
        return v.transpose(1, 0, 2).reshape(v.shape[1], -1)

    def total(a, b):
        return a.astype(jnp.float32) + jnp.sum(b.astype(jnp.float32), axis=0)

    return flat(out), flat(inp), total(ga_u, gb_u), total(ga_d, gb_d)


def solution(mesh):
    sizes = (mesh.shape["tensor"], mesh.shape["fsdp"] // 2, mesh.shape["dp"])
    in_specs = (
        P(("dp", "fsdp"), "tensor"),
        P(("dp", "fsdp"), "tensor"),
        P(("fsdp", "tensor"), None, None),
        P(("fsdp", "tensor"), None, None),
        P(None, "tensor"),
        P(None, "tensor"),
        P(None, "tensor"),
        P(None, "tensor"),
    )
    out_specs = (
        P(("dp", "fsdp"), "tensor"),
        P(("dp", "fsdp"), "tensor"),
        P(("fsdp", "tensor"), None, None),
        P(("fsdp", "tensor"), None, None),
    )
    return jax.shard_map(
        functools.partial(body, sizes), mesh=mesh, in_specs=in_specs, out_specs=out_specs,
        check_vma=False,
    )
```

```python
import functools
from itertools import zip_longest

import jax
import jax.numpy as jnp
from jax import lax
from jax.experimental import pallas as pl
from jax.experimental.pallas import tpu as pltpu
from jax.sharding import PartitionSpec as P

MESH = pl.DeviceIdType.MESH
COL_TILES = 8
PIECES = 8

inv_root_two = 0.7071067811865476
inv_root_tau = 0.3989422804014327


def gelu_parts(values):
    normal_cdf = 0.5 * (1.0 + lax.erf(values * inv_root_two))
    density = inv_root_tau * jnp.exp(-0.5 * values * values)
    return (values * normal_cdf, normal_cdf + values * density)


def remote(src, dst, send_sem, recv_sem, where):
    return pltpu.make_async_remote_copy(
        src_ref=src, dst_ref=dst, send_sem=send_sem, recv_sem=recv_sem,
        device_id=where, device_id_type=MESH,
    )


def place(sizes):
    n, chips, replicas = sizes
    z = lax.axis_index("tensor")
    f = lax.axis_index("fsdp")
    y = lax.axis_index("dp")
    return z, f // 2, f % 2, y


def enter(sizes):
    n, chips, replicas = sizes
    z, r, c, y = place(sizes)
    barrier = pltpu.get_barrier_semaphore()

    def greet(where):
        pl.semaphore_signal(barrier, inc=1, device_id=where, device_id_type=MESH)

    @pl.when(z < n - 1)
    def _():
        greet({"tensor": z + 1})

    @pl.when(z > 0)
    def _():
        greet({"tensor": z - 1})

    greet({"fsdp": r * 2 + 1 - c})
    for d in range(1, chips):
        greet({"fsdp": lax.rem(r + d, chips) * 2 + c})
    for e in range(1, replicas):
        greet({"dp": lax.rem(y + e, replicas)})
    sides = jnp.where(z < n - 1, 1, 0) + jnp.where(z > 0, 1, 0)
    pl.semaphore_wait(barrier, sides + 1 + (chips - 1) + (replicas - 1))


def gather_kernel(
    sizes, act, cot, up, down, x_all, c_all, u_all, d_all,
    own_x, own_c, own_u, own_d,
    load_sem, keep_sem, zs_sem, zr_sem, xs_sem, xr_sem, ys_sem, yr_sem, cs_sem, cr_sem,
):
    n, chips, replicas = sizes
    z, r, c, y = place(sizes)
    f = r * 2 + c
    blocks = own_x.shape[0]
    per = up.shape[0]
    part = per // replicas
    features = ((act, own_x, x_all), (cot, own_c, c_all))
    weights = ((up, own_u, u_all), (down, own_d, d_all))

    loads = []
    for a, (src, own, _) in enumerate(features):
        for b in range(blocks):
            copy = pltpu.make_async_copy(
                src.at[:, pl.ds(b * 128, 128)], own.at[b], load_sem.at[a, b]
            )
            copy.start()
            loads.append(copy)
    for a, (src, own, _) in enumerate(weights):
        copy = pltpu.make_async_copy(src, own, load_sem.at[2 + a, 0])
        copy.start()
    enter(sizes)
    for copy in loads:
        copy.wait()

    def shard(full, s):
        return full.at[pl.ds(s * blocks, blocks)]

    def line(a, s, way, source):
        _, own, full = features[a]
        k = 0 if way > 0 else 1
        mine = own if source else shard(full, z - way * s)
        return remote(
            mine, shard(full, z - way * s), zs_sem.at[a, k, s], zr_sem.at[a, k, s],
            {"tensor": z + way},
        )

    def can_send(way):
        return z < n - 1 if way > 0 else z > 0

    def has(s, way):
        return z - s >= 0 if way > 0 else z + s <= n - 1

    for a in range(2):
        for way in (1, -1):

            @pl.when(can_send(way))
            def _():
                line(a, 0, way, True).start()

    def tile_range(full, r_of, c_of, q):
        return full.at[pl.ds((r_of * 2 + c_of) * per + q * part, part)]

    def x_copy(a, d):
        src = weights[a][0].at[pl.ds(y * part, part)]
        return remote(
            src, tile_range(weights[a][2], r, c, y), xs_sem.at[a, d], xr_sem.at[a, d],
            {"fsdp": lax.rem(r + d, chips) * 2 + c},
        )

    for a in range(2):
        for d in range(1, chips):
            x_copy(a, d).start()

    def own_core(a):
        full = weights[a][2]
        return remote(
            weights[a][0], full.at[pl.ds(f * per, per)], cs_sem.at[a, 0, 0], cr_sem.at[a, 0, 0],
            {"fsdp": r * 2 + 1 - c},
        )

    for a in range(2):
        own_core(a).start()

    keeps = []
    for a, (_, own, full) in enumerate(features):
        keeps.append(pltpu.make_async_copy(own, shard(full, z), keep_sem.at[a]))
    for a, (src, own, full) in enumerate(weights):
        pltpu.make_async_copy(src, own, load_sem.at[2 + a, 0]).wait()
        keeps.append(
            pltpu.make_async_copy(own, full.at[pl.ds(f * per, per)], keep_sem.at[2 + a])
        )
    for copy in keeps:
        copy.start()

    def y_copy(a, d, e):
        piece = tile_range(weights[a][2], lax.rem(r - d + chips, chips), c, y)
        return remote(
            piece, piece, ys_sem.at[a, d, e], yr_sem.at[a, d, e],
            {"dp": lax.rem(y + e, replicas)},
        )

    def core_copy(a, d, e):
        q = lax.rem(y - e + replicas, replicas)
        piece = tile_range(weights[a][2], lax.rem(r - d + chips, chips), c, q)
        return remote(
            piece, piece, cs_sem.at[a, d, e], cr_sem.at[a, d, e], {"fsdp": r * 2 + 1 - c}
        )

    def z_event(s):
        for a in range(2):
            for way in (1, -1):

                @pl.when(has(s, way))
                def _():
                    line(a, s - 1, way, False).wait_recv()

                    if s < n - 1:

                        @pl.when(can_send(way))
                        def _():
                            line(a, s, way, False).start()

    def x_event(a):
        for d in range(1, chips):
            x_copy(a, d).wait_recv()
            for e in range(1, replicas):
                y_copy(a, d, e).start()
            core_copy(a, d, 0).start()

    def y_event(a):
        for d in range(1, chips):
            for e in range(1, replicas):
                y_copy(a, d, e).wait_recv()
                core_copy(a, d, e).start()

    tile_events = [
        lambda: x_event(0),
        lambda: (x_event(1), y_event(0)),
        lambda: y_event(1),
    ]
    z_events = [functools.partial(z_event, s) for s in range(1, n)]
    for first, second in zip_longest(z_events, tile_events):
        if first is not None:
            first()
        if second is not None:
            second()

    for copy in keeps:
        copy.wait()
    for a in range(2):
        own_core(a).wait()
        for d in range(1, chips):
            x_copy(a, d).wait_send()
            core_copy(a, d, 0).wait()
            for e in range(1, replicas):
                y_copy(a, d, e).wait_send()
                core_copy(a, d, e).wait()
        for way in (1, -1):
            for s in range(n - 1):

                @pl.when(jnp.logical_and(can_send(way), has(s, way)))
                def _():
                    line(a, s, way, s == 0).wait_send()


def gather(sizes, activations, cotangent, up_tiles, down_tiles):
    n, chips, replicas = sizes
    rows, wide = activations.shape
    blocks = wide // 128
    per = up_tiles.shape[0]
    kind = jnp.bfloat16
    dma = pltpu.SemaphoreType.DMA
    anywhere = pl.BlockSpec(memory_space=pl.ANY)
    return pl.pallas_call(
        functools.partial(gather_kernel, sizes),
        out_shape=(
            jax.ShapeDtypeStruct((n * blocks, rows, 128), kind),
            jax.ShapeDtypeStruct((n * blocks, rows, 128), kind),
            jax.ShapeDtypeStruct((2 * chips * per, 128, 128), kind),
            jax.ShapeDtypeStruct((2 * chips * per, 128, 128), kind),
        ),
        in_specs=[anywhere] * 4,
        out_specs=(anywhere,) * 4,
        scratch_shapes=[
            pltpu.VMEM((blocks, rows, 128), kind),
            pltpu.VMEM((blocks, rows, 128), kind),
            pltpu.VMEM((per, 128, 128), kind),
            pltpu.VMEM((per, 128, 128), kind),
            dma((4, blocks)),
            dma((4,)),
            dma((2, 2, n)),
            dma((2, 2, n)),
            dma((2, chips)),
            dma((2, chips)),
            dma((2, chips, replicas)),
            dma((2, chips, replicas)),
            dma((2, chips, replicas)),
            dma((2, chips, replicas)),
        ],
        compiler_params=pltpu.CompilerParams(collective_id=0, has_side_effects=True),
        name="gather_all",
    )(activations, cotangent, up_tiles, down_tiles)


def mm(a, b, ca, cb):
    return lax.dot_general(a, b, (((ca,), (cb,)), ((), ())), preferred_element_type=jnp.float32)


def forward_kernel(hidden_blocks, uo, uf, x, u, hidden, slope, xt):
    @pl.loop(0, x.shape[0])
    def _(b):
        xt[b] = x[b].T

    @pl.loop(0, hidden_blocks)
    def _(h):
        first = h * COL_TILES
        pre = mm(x[uf[first]], u[uo[first]], 1, 0)
        for k in range(1, COL_TILES):
            pre += mm(x[uf[first + k]], u[uo[first + k]], 1, 0)
        value, tangent = gelu_parts(pre)
        hidden[h] = value.astype(jnp.bfloat16)
        slope[h] = tangent


def forward(order, far, x, u):
    vmem = pl.BlockSpec(memory_space=pltpu.VMEM)
    smem = pl.BlockSpec(memory_space=pltpu.SMEM)
    hidden_blocks = u.shape[0] // COL_TILES
    rows = x.shape[1]
    return pl.pallas_call(
        functools.partial(forward_kernel, hidden_blocks),
        out_shape=(
            jax.ShapeDtypeStruct((hidden_blocks, rows, 128), jnp.bfloat16),
            jax.ShapeDtypeStruct((hidden_blocks, rows, 128), jnp.float32),
            jax.ShapeDtypeStruct((x.shape[0], 128, rows), jnp.bfloat16),
        ),
        in_specs=[smem] * 2 + [vmem] * 2,
        out_specs=(vmem,) * 3,
        compiler_params=pltpu.CompilerParams(vmem_limit_bytes=60 * 1024 * 1024),
        name="forward_work",
    )(order, far, x, u)


def add_into(target, terms):
    @pl.loop(0, target.shape[0])
    def _(b):
        total = terms[0][b].astype(jnp.float32)
        for term in terms[1:]:
            total += term[b].astype(jnp.float32)
        target[b] = total.astype(target.dtype)


def reduce_kernel(
    sizes, do, df, up_rows, up_cols, down_rows, down_cols,
    far_order_u, far_near_u, far_first_u, last_u, far_order_d, far_near_d, far_first_d, last_d,
    hidden, slope, xt, cot, up, down,
    out, inp, ga_u, ga_d, gb_u, gb_d,
    u_all, d_all, hidden_t, pre_grad, run, acc, parts_o, parts_i,
    held_r, held_l, stage, core_in, x_in,
    load_sem, keep_sem, zs_sem, zr_sem, cs_sem, cr_sem, xs_sem, xr_sem, ys_sem, yr_sem,
):
    n, chips, replicas = sizes
    z, r, c, y = place(sizes)
    blocks = out.shape[0]
    hidden_blocks = hidden.shape[0]
    per = ga_u.shape[0]
    total_tiles = u_all.shape[0]
    size = per // PIECES
    parts = (parts_o, parts_i)
    outs = (out, inp)
    sums = (ga_d, ga_u)
    others = (gb_d, gb_u)
    held = (held_r, held_l)

    load_d = pltpu.make_async_copy(down, d_all, load_sem.at[0])
    load_u = pltpu.make_async_copy(up, u_all, load_sem.at[1])
    load_d.start()
    load_u.start()
    enter(sizes)

    @pl.loop(0, hidden_blocks)
    def _(h):
        hidden_t[h] = hidden[h].T

    def term(a, j):
        if a == 0:
            return mm(hidden_t[down_rows[j]], cot[down_cols[j]], 1, 0)
        return mm(xt[up_rows[j]], pre_grad[up_cols[j]], 1, 0)

    def first_tile(q, c_of, k):
        return (q * 2 + c_of) * per + k * size

    width = 4 if size % 4 == 0 else 1

    def staged(a, k, q):
        at = (k * chips + q) * size
        return (stage if a == 0 else d_all).at[pl.ds(at, size)]

    def core_copy(a, k, q):
        return remote(
            staged(a, k, q), core_in.at[a, q, pl.ds(k * size, size)],
            cs_sem.at[a, k, q], cr_sem.at[a, k, q], {"fsdp": r * 2 + 1 - c},
        )

    def hand_over(a, k):
        for q in range(chips):
            target = staged(a, k, q)

            @pl.loop(0, size // width)
            def _(i):
                values = [term(a, first_tile(q, 1 - c, k) + i * width + w) for w in range(width)]
                for w in range(width):
                    target[i * width + w] = values[w].astype(jnp.bfloat16)

        for q in range(chips):
            core_copy(a, k, q).start()

    def sum_with(a, k, q, target, terms):
        @pl.loop(0, size // width)
        def _(i):
            values = [term(a, first_tile(q, c, k) + i * width + w) for w in range(width)]
            for w in range(width):
                total = values[w].astype(jnp.bfloat16).astype(jnp.float32)
                for other in terms:
                    total += other[i * width + w].astype(jnp.float32)
                target[i * width + w] = total.astype(jnp.bfloat16)

    def x_copy(a, k, d):
        q = lax.rem(r + d, chips)
        return remote(
            core_in.at[a, q, pl.ds(k * size, size)], x_in.at[a, d - 1, pl.ds(k * size, size)],
            xs_sem.at[a, k, d], xr_sem.at[a, k, d], {"fsdp": q * 2 + c},
        )

    def done_piece(a, k):
        return core_in.at[a, r, pl.ds(k * size, size)]

    def y_copy(a, k, e):
        return remote(
            done_piece(a, k), others[a].at[e - 1, pl.ds(k * size, size)],
            ys_sem.at[a, k, e], yr_sem.at[a, k, e], {"dp": lax.rem(y + e, replicas)},
        )

    def keep_copy(a, k):
        return pltpu.make_async_copy(
            done_piece(a, k), sums[a].at[pl.ds(k * size, size)], keep_sem.at[a, k]
        )

    def feed(a, k):
        for d in range(1, chips):
            q = lax.rem(r + d, chips)
            core_copy(a, k, q).wait_recv()
            mine = core_in.at[a, q, pl.ds(k * size, size)]
            sum_with(a, k, q, mine, [mine])
            x_copy(a, k, d).start()

    def x_event(a, k):
        core_copy(a, k, r).wait_recv()
        for d in range(1, chips):
            x_copy(a, k, d).wait_recv()
        mine = done_piece(a, k)
        sum_with(
            a, k, r, mine,
            [mine] + [x_in.at[a, d - 1, pl.ds(k * size, size)] for d in range(1, chips)],
        )
        for e in range(1, replicas):
            y_copy(a, k, e).start()
        keep_copy(a, k).start()

    def shard(ref, s):
        return ref.at[pl.ds(s * blocks, blocks)]

    def line(a, i, way, source):
        s = n - 1 - i if way > 0 else i
        k = 0 if way > 0 else 1
        src = shard(parts[a], s) if source else held[k].at[a, i]
        return remote(
            src, held[k].at[a, i], zs_sem.at[a, k, i], zr_sem.at[a, k, i], {"tensor": z + way}
        )

    def edge(way):
        return z == 0 if way > 0 else z == n - 1

    def sends(i, way):
        return n - 1 - i > z if way > 0 else i < z

    def z_start(a):
        for i in range(n - 1):
            for way in (1, -1):

                @pl.when(edge(way))
                def _():
                    line(a, i, way, True).start()

    def z_event(t, a):
        for way in (1, -1):
            i = t - z if way > 0 else t - (n - 1 - z)
            s = n - 1 - i if way > 0 else i
            k = 0 if way > 0 else 1
            on_way = jnp.logical_and(i >= 0, sends(i, way))

            @pl.when(jnp.logical_and(on_way, jnp.logical_not(edge(way))))
            def _():
                line(a, i, way, False).wait_recv()
                add_into(held[k].at[a, i], (held[k].at[a, i], shard(parts[a], s)))
                line(a, i, way, False).start()

    def slope_part(g):
        span = hidden_blocks // 4

        @pl.loop(g * span, (g + 1) * span)
        def _(h):
            first = h * COL_TILES
            value = mm(cot[df[first]], d_all[do[first]], 1, 1)
            for k in range(1, COL_TILES):
                value += mm(cot[df[first + k]], d_all[do[first + k]], 1, 1)
            pre_grad[h] = (value * slope[h]).astype(jnp.bfloat16)

    def run_part(a, g):
        order, near, fresh = (
            (far_order_d, far_near_d, far_first_d) if a == 0 else (far_order_u, far_near_u, far_first_u)
        )
        left, right, cut = (hidden, d_all, 0) if a == 0 else (pre_grad, u_all, 1)
        span = total_tiles // 4 // 8
        if g == 0:
            acc[...] = jnp.zeros_like(acc)

        @pl.loop(g * span, (g + 1) * span)
        def _(b):
            spots = [b * 8 + k for k in range(8)]
            products = [mm(left[near[i]], right[order[i]], 1, cut) for i in spots]
            total = acc[...]
            for i, product in zip(spots, products):
                total = jnp.where(fresh[i] == 1, 0.0, total) + product
                run[i] = total.astype(jnp.bfloat16)
            acc[...] = total

    def settle(a):
        last = last_d if a == 0 else last_u
        target = parts[a]

        @pl.loop(0, target.shape[0])
        def _(b):
            spot = last[b]
            found = run[jnp.maximum(spot, 0)]
            target[b] = jnp.where(spot >= 0, found, jnp.zeros_like(found))

        z_start(a)

    for k in range(PIECES):
        hand_over(0, k)
    for k in range(PIECES):
        feed(0, k)
    load_d.wait()
    load_u.wait()
    work = (
        [functools.partial(slope_part, g) for g in range(4)]
        + [functools.partial(run_part, 0, g) for g in range(4)]
        + [functools.partial(settle, 0)]
        + [functools.partial(run_part, 1, g) for g in range(4)]
        + [functools.partial(settle, 1)]
    )
    slots = [(t, a) for a in range(2) for t in range(1, n - 1)]
    pieces = [(a, k) for a in range(2) for k in range(PIECES)]
    handed = 0
    fed = 0
    for i, piece in enumerate(pieces):
        for step in work[:3]:
            step()
        work = work[3:]
        if not work and handed < PIECES:
            hand_over(1, handed)
            handed += 1
        if not work and handed >= 2 and fed < handed - 1:
            feed(1, fed)
            fed += 1
        if i >= 5 and i % 2 == 1 and slots:
            z_event(*slots.pop(0))
        if i == PIECES - 1:
            while handed < PIECES:
                hand_over(1, handed)
                handed += 1
        if i >= PIECES - 1 and fed < PIECES:
            feed(1, fed)
            fed += 1
        x_event(*piece)
    for slot in slots:
        z_event(*slot)

    for a in range(2):
        mine = shard(parts[a], z)

        @pl.when(z > 0)
        def _():
            line(a, n - 1 - z, 1, False).wait_recv()

        @pl.when(z < n - 1)
        def _():
            line(a, z, -1, False).wait_recv()

        @pl.when(z == 0)
        def _():
            add_into(outs[a], (mine, held_l.at[a, z]))

        @pl.when(z == n - 1)
        def _():
            add_into(outs[a], (mine, held_r.at[a, n - 1 - z]))

        @pl.when(jnp.logical_and(z > 0, z < n - 1))
        def _():
            add_into(outs[a], (mine, held_r.at[a, n - 1 - z], held_l.at[a, z]))

        for i in range(n - 1):
            for way in (1, -1):

                @pl.when(sends(i, way))
                def _():
                    line(a, i, way, False).wait_send()

        for k in range(PIECES):
            for q in range(chips):
                core_copy(a, k, q).wait_send()
            for d in range(1, chips):
                x_copy(a, k, d).wait_send()
            keep_copy(a, k).wait()
            for e in range(1, replicas):
                y_copy(a, k, e).wait()


def reduce(sizes, tables, hidden, slope, xt, cot, up, down):
    n, chips, replicas = sizes
    blocks = cot.shape[0] // n
    rows = cot.shape[1]
    per = up.shape[0] // (2 * chips)
    kind = jnp.bfloat16
    dma = pltpu.SemaphoreType.DMA
    vmem = pl.BlockSpec(memory_space=pltpu.VMEM)
    smem = pl.BlockSpec(memory_space=pltpu.SMEM)
    anywhere = pl.BlockSpec(memory_space=pl.ANY)
    return pl.pallas_call(
        functools.partial(reduce_kernel, sizes),
        out_shape=(
            [jax.ShapeDtypeStruct((blocks, rows, 128), kind)] * 2
            + [jax.ShapeDtypeStruct((per, 128, 128), kind)] * 2
            + [jax.ShapeDtypeStruct((replicas - 1, per, 128, 128), kind)] * 2
        ),
        in_specs=[smem] * len(tables) + [vmem] * 4 + [anywhere] * 2,
        out_specs=[vmem] * 2 + [anywhere] * 4,
        scratch_shapes=[
            pltpu.VMEM(up.shape, kind),
            pltpu.VMEM(down.shape, kind),
            pltpu.VMEM((hidden.shape[0], 128, rows), kind),
            pltpu.VMEM(hidden.shape, kind),
            pltpu.VMEM((up.shape[0], rows, 128), kind),
            pltpu.VMEM((rows, 128), jnp.float32),
            pltpu.VMEM(cot.shape, kind),
            pltpu.VMEM(cot.shape, kind),
            pltpu.VMEM((2, n - 1, blocks, rows, 128), kind),
            pltpu.VMEM((2, n - 1, blocks, rows, 128), kind),
            pltpu.VMEM((chips * per, 128, 128), kind),
            pltpu.VMEM((2, chips, per, 128, 128), kind),
            pltpu.VMEM((2, max(chips - 1, 1), per, 128, 128), kind),
            dma((2,)),
            dma((2, PIECES)),
            dma((2, 2, n)),
            dma((2, 2, n)),
            dma((2, PIECES, chips)),
            dma((2, PIECES, chips)),
            dma((2, PIECES, chips)),
            dma((2, PIECES, chips)),
            dma((2, PIECES, replicas)),
            dma((2, PIECES, replicas)),
        ],
        compiler_params=pltpu.CompilerParams(
            collective_id=1, has_side_effects=True, vmem_limit_bytes=67043328
        ),
        name="reduce_all",
    )(*tables, hidden, slope, xt, cot, up, down)


def tables_of(near, far, model_blocks):
    count = near.shape[0]
    at = lax.iota(jnp.int32, count)
    before = at[:, None] < at[None, :]
    equal = far[:, None] == far[None, :]
    spot = near * COL_TILES + jnp.sum(((near[:, None] == near[None, :]) & before).astype(jnp.int32), axis=0)
    here = spot[:, None] == at[None, :]
    packed = jnp.sum(jnp.where(here, (at * model_blocks + far)[:, None], 0), axis=0)
    rank = jnp.sum((equal & before).astype(jnp.int32), axis=0)
    place_of = rank + jnp.sum((far[:, None] < far[None, :]).astype(jnp.int32), axis=0)
    there = place_of[:, None] == at[None, :]
    code = (at * count + near) * 2 + (rank == 0)
    far_packed = jnp.sum(jnp.where(there, code[:, None], 0), axis=0)
    block = lax.iota(jnp.int32, model_blocks)
    matches = far[:, None] == block[None, :]
    until = jnp.sum((far[:, None] <= block[None, :]).astype(jnp.int32), axis=0)
    last = jnp.where(jnp.any(matches, axis=0), until - 1, -1)
    far_code = far_packed // 2
    return (
        packed // model_blocks, packed % model_blocks,
        far_code // count, far_code % count, far_packed % 2, last,
    )


def body(sizes, activations, cotangent, up_tiles, down_tiles, up_rows, up_cols, down_rows, down_cols):
    ur, uc, dr, dc = (v[:, 0] for v in (up_rows, up_cols, down_rows, down_cols))
    model_blocks = sizes[0] * activations.shape[1] // 128
    sort = jax.vmap(functools.partial(tables_of, model_blocks=model_blocks))
    order, far, far_order, far_near, far_first, last = sort(jnp.stack([uc, dr]), jnp.stack([ur, dc]))
    x, cot, up, down = gather(sizes, activations, cotangent, up_tiles, down_tiles)
    hidden, slope, xt = forward(order[0], far[0], x, up)
    tables = (
        order[1], far[1], ur, uc, dr, dc,
        far_order[0], far_near[0], far_first[0], last[0],
        far_order[1], far_near[1], far_first[1], last[1],
    )
    out, inp, ga_u, ga_d, gb_u, gb_d = reduce(sizes, tables, hidden, slope, xt, cot, up, down)

    def flat(v):
        return v.transpose(1, 0, 2).reshape(v.shape[1], -1)

    def total(a, b):
        return a.astype(jnp.float32) + jnp.sum(b.astype(jnp.float32), axis=0)

    return flat(out), flat(inp), total(ga_u, gb_u), total(ga_d, gb_d)


def solution(mesh):
    sizes = (mesh.shape["tensor"], mesh.shape["fsdp"] // 2, mesh.shape["dp"])
    in_specs = (
        P(("dp", "fsdp"), "tensor"),
        P(("dp", "fsdp"), "tensor"),
        P(("fsdp", "tensor"), None, None),
        P(("fsdp", "tensor"), None, None),
        P(None, "tensor"),
        P(None, "tensor"),
        P(None, "tensor"),
        P(None, "tensor"),
    )
    out_specs = (
        P(("dp", "fsdp"), "tensor"),
        P(("dp", "fsdp"), "tensor"),
        P(("fsdp", "tensor"), None, None),
        P(("fsdp", "tensor"), None, None),
    )
    return jax.shard_map(
        functools.partial(body, sizes), mesh=mesh, in_specs=in_specs, out_specs=out_specs,
        check_vma=False,
    )
```

```python
import functools

import jax
import jax.numpy as jnp
from jax import lax
from jax.experimental import pallas as pl
from jax.experimental.pallas import tpu as pltpu
from jax.sharding import PartitionSpec as P

MESH = pl.DeviceIdType.MESH
COL_TILES = 8
PIECES = 8

inv_root_two = 0.7071067811865476
inv_root_tau = 0.3989422804014327


def gelu_parts(values):
    normal_cdf = 0.5 * (1.0 + lax.erf(values * inv_root_two))
    density = inv_root_tau * jnp.exp(-0.5 * values * values)
    return (values * normal_cdf, normal_cdf + values * density)


def remote(src, dst, send_sem, recv_sem, where):
    return pltpu.make_async_remote_copy(
        src_ref=src, dst_ref=dst, send_sem=send_sem, recv_sem=recv_sem,
        device_id=where, device_id_type=MESH,
    )


def place(sizes):
    n, chips, replicas = sizes
    z = lax.axis_index("tensor")
    f = lax.axis_index("fsdp")
    y = lax.axis_index("dp")
    return z, f // 2, f % 2, y


def enter(sizes):
    n, chips, replicas = sizes
    z, r, c, y = place(sizes)
    barrier = pltpu.get_barrier_semaphore()

    def greet(where):
        pl.semaphore_signal(barrier, inc=1, device_id=where, device_id_type=MESH)

    @pl.when(z < n - 1)
    def _():
        greet({"tensor": z + 1})

    @pl.when(z > 0)
    def _():
        greet({"tensor": z - 1})

    greet({"fsdp": r * 2 + 1 - c})
    for d in range(1, chips):
        greet({"fsdp": lax.rem(r + d, chips) * 2 + c})
    for e in range(1, replicas):
        greet({"dp": lax.rem(y + e, replicas)})
    sides = jnp.where(z < n - 1, 1, 0) + jnp.where(z > 0, 1, 0)
    pl.semaphore_wait(barrier, sides + 1 + (chips - 1) + (replicas - 1))


def gather_kernel(
    sizes, uo, uf, act, cot, up, down, c_all, u_all, d_all, hidden, slope, xt,
    x_all, u_held, own_c, own_u, own_d,
    load_sem, keep_sem, zs_sem, zr_sem, xs_sem, xr_sem, ys_sem, yr_sem, cs_sem, cr_sem,
):
    n, chips, replicas = sizes
    z, r, c, y = place(sizes)
    f = r * 2 + c
    blocks = own_c.shape[0]
    per = up.shape[0]
    part = per // replicas
    own_x = x_all.at[pl.ds(z * blocks, blocks)]
    features = ((act, own_x, x_all), (cot, own_c, c_all))
    weights = ((up, own_u, u_all), (down, own_d, d_all))

    loads = []
    for a, (src, own, _) in enumerate(features):
        for b in range(blocks):
            copy = pltpu.make_async_copy(
                src.at[:, pl.ds(b * 128, 128)], own.at[b], load_sem.at[a, b]
            )
            copy.start()
            loads.append(copy)
    for a, (src, own, _) in enumerate(weights):
        copy = pltpu.make_async_copy(src, own, load_sem.at[2 + a, 0])
        copy.start()
    enter(sizes)
    for copy in loads:
        copy.wait()

    def shard(full, s):
        return full.at[pl.ds(s * blocks, blocks)]

    def line(a, s, way, source):
        _, own, full = features[a]
        k = 0 if way > 0 else 1
        mine = own if source else shard(full, z - way * s)
        return remote(
            mine, shard(full, z - way * s), zs_sem.at[a, k, s], zr_sem.at[a, k, s],
            {"tensor": z + way},
        )

    def can_send(way):
        return z < n - 1 if way > 0 else z > 0

    def has(s, way):
        return z - s >= 0 if way > 0 else z + s <= n - 1

    def z_start(a):
        for way in (1, -1):

            @pl.when(can_send(way))
            def _():
                line(a, 0, way, True).start()

    z_start(0)

    def tile_range(full, r_of, c_of, q):
        return full.at[pl.ds((r_of * 2 + c_of) * per + q * part, part)]

    def x_copy(a, d):
        src = weights[a][0].at[pl.ds(y * part, part)]
        return remote(
            src, tile_range(weights[a][2], r, c, y), xs_sem.at[a, d], xr_sem.at[a, d],
            {"fsdp": lax.rem(r + d, chips) * 2 + c},
        )

    for a in range(2):
        for d in range(1, chips):
            x_copy(a, d).start()

    def own_core(a):
        full = weights[a][2]
        return remote(
            weights[a][0], full.at[pl.ds(f * per, per)], cs_sem.at[a, 0, 0], cr_sem.at[a, 0, 0],
            {"fsdp": r * 2 + 1 - c},
        )

    for a in range(2):
        own_core(a).start()

    keeps = []
    keeps.append(pltpu.make_async_copy(own_c, shard(c_all, z), keep_sem.at[0]))
    for a, (src, own, full) in enumerate(weights):
        pltpu.make_async_copy(src, own, load_sem.at[2 + a, 0]).wait()
        keeps.append(
            pltpu.make_async_copy(own, full.at[pl.ds(f * per, per)], keep_sem.at[1 + a])
        )
    for copy in keeps:
        copy.start()

    def y_copy(a, d, e):
        piece = tile_range(weights[a][2], lax.rem(r - d + chips, chips), c, y)
        return remote(
            piece, piece, ys_sem.at[a, d, e], yr_sem.at[a, d, e],
            {"dp": lax.rem(y + e, replicas)},
        )

    def core_copy(a, d, e):
        q = lax.rem(y - e + replicas, replicas)
        piece = tile_range(weights[a][2], lax.rem(r - d + chips, chips), c, q)
        return remote(
            piece, piece, cs_sem.at[a, d, e], cr_sem.at[a, d, e], {"fsdp": r * 2 + 1 - c}
        )

    def z_event(a, s):
        for way in (1, -1):

            @pl.when(has(s, way))
            def _():
                line(a, s - 1, way, False).wait_recv()

                if s < n - 1:

                    @pl.when(can_send(way))
                    def _():
                        line(a, s, way, False).start()

    def x_event(a):
        for d in range(1, chips):
            x_copy(a, d).wait_recv()
            for e in range(1, replicas):
                y_copy(a, d, e).start()
            core_copy(a, d, 0).start()

    def y_event(a):
        for d in range(1, chips):
            for e in range(1, replicas):
                y_copy(a, d, e).wait_recv()
                core_copy(a, d, e).start()

    load_up = pltpu.make_async_copy(u_all, u_held, load_sem.at[4, 0])

    def fetch_up():
        keeps[1].wait()
        own_core(0).wait_recv()
        for d in range(1, chips):
            for e in range(replicas):
                core_copy(0, d, e).wait_recv()
        load_up.start()
        load_up.wait()

    def turn():
        @pl.loop(0, x_all.shape[0])
        def _(b):
            xt[b] = x_all[b].T

    hidden_blocks = hidden.shape[0]

    def forward_part(g):
        span = hidden_blocks // 4

        @pl.loop(g * span, (g + 1) * span)
        def _(h):
            first = h * COL_TILES
            pre = mm(x_all[uf[first]], u_held[uo[first]], 1, 0)
            for k in range(1, COL_TILES):
                pre += mm(x_all[uf[first + k]], u_held[uo[first + k]], 1, 0)
            value, tangent = gelu_parts(pre)
            hidden[h] = value.astype(jnp.bfloat16)
            slope[h] = tangent

    for s in range(1, n - 1):
        z_event(0, s)
    z_start(1)
    x_event(0)
    z_event(0, n - 1)
    turn()
    x_event(1)
    y_event(0)
    later = [functools.partial(z_event, 1, s) for s in range(1, n - 1)]
    later.pop(0)()
    fetch_up()
    forward_part(0)
    forward_part(1)
    for event in later:
        event()
    forward_part(2)
    y_event(1)
    forward_part(3)
    z_event(1, n - 1)

    keeps[0].wait()
    keeps[2].wait()
    own_core(1).wait_recv()
    for a in range(2):
        own_core(a).wait_send()
        for d in range(1, chips):
            x_copy(a, d).wait_send()
            for e in range(replicas):
                core_copy(a, d, e).wait_send()
                if a == 1:
                    core_copy(a, d, e).wait_recv()
            for e in range(1, replicas):
                y_copy(a, d, e).wait_send()
        for way in (1, -1):
            for s in range(n - 1):

                @pl.when(jnp.logical_and(can_send(way), has(s, way)))
                def _():
                    line(a, s, way, s == 0).wait_send()


def gather(sizes, order, far, activations, cotangent, up_tiles, down_tiles):
    n, chips, replicas = sizes
    rows, wide = activations.shape
    blocks = wide // 128
    per = up_tiles.shape[0]
    hidden_blocks = 2 * chips * per // COL_TILES
    kind = jnp.bfloat16
    dma = pltpu.SemaphoreType.DMA
    vmem = pl.BlockSpec(memory_space=pltpu.VMEM)
    smem = pl.BlockSpec(memory_space=pltpu.SMEM)
    anywhere = pl.BlockSpec(memory_space=pl.ANY)
    return pl.pallas_call(
        functools.partial(gather_kernel, sizes),
        out_shape=(
            jax.ShapeDtypeStruct((n * blocks, rows, 128), kind),
            jax.ShapeDtypeStruct((2 * chips * per, 128, 128), kind),
            jax.ShapeDtypeStruct((2 * chips * per, 128, 128), kind),
            jax.ShapeDtypeStruct((hidden_blocks, rows, 128), kind),
            jax.ShapeDtypeStruct((hidden_blocks, rows, 128), jnp.float32),
            jax.ShapeDtypeStruct((n * blocks, 128, rows), kind),
        ),
        in_specs=[smem] * 2 + [anywhere] * 4,
        out_specs=(anywhere,) * 3 + (vmem,) * 3,
        scratch_shapes=[
            pltpu.VMEM((n * blocks, rows, 128), kind),
            pltpu.VMEM((2 * chips * per, 128, 128), kind),
            pltpu.VMEM((blocks, rows, 128), kind),
            pltpu.VMEM((per, 128, 128), kind),
            pltpu.VMEM((per, 128, 128), kind),
            dma((5, blocks)),
            dma((3,)),
            dma((2, 2, n)),
            dma((2, 2, n)),
            dma((2, chips)),
            dma((2, chips)),
            dma((2, chips, replicas)),
            dma((2, chips, replicas)),
            dma((2, chips, replicas)),
            dma((2, chips, replicas)),
        ],
        compiler_params=pltpu.CompilerParams(
            collective_id=0, has_side_effects=True, vmem_limit_bytes=60 * 1024 * 1024
        ),
        name="gather_all",
    )(order, far, activations, cotangent, up_tiles, down_tiles)


def mm(a, b, ca, cb):
    return lax.dot_general(a, b, (((ca,), (cb,)), ((), ())), preferred_element_type=jnp.float32)


def add_into(target, terms):
    @pl.loop(0, target.shape[0])
    def _(b):
        total = terms[0][b].astype(jnp.float32)
        for term in terms[1:]:
            total += term[b].astype(jnp.float32)
        target[b] = total.astype(target.dtype)


def reduce_kernel(
    sizes, do, df, up_rows, up_cols, down_rows, down_cols,
    far_order_u, far_near_u, far_first_u, last_u, far_order_d, far_near_d, far_first_d, last_d,
    hidden, slope, xt, cot, up, down,
    out, inp, ga_u, ga_d, gb_u, gb_d,
    u_all, d_all, hidden_t, pre_grad, run, acc, parts_o, parts_i,
    held_r, held_l, stage, core_in, x_in,
    load_sem, keep_sem, zs_sem, zr_sem, cs_sem, cr_sem, xs_sem, xr_sem, ys_sem, yr_sem,
):
    n, chips, replicas = sizes
    z, r, c, y = place(sizes)
    blocks = out.shape[0]
    hidden_blocks = hidden.shape[0]
    per = ga_u.shape[0]
    total_tiles = u_all.shape[0]
    size = per // PIECES
    parts = (parts_o, parts_i)
    outs = (out, inp)
    sums = (ga_d, ga_u)
    others = (gb_d, gb_u)
    held = (held_r, held_l)

    load_d = pltpu.make_async_copy(down, d_all, load_sem.at[0])
    load_u = pltpu.make_async_copy(up, u_all, load_sem.at[1])
    load_d.start()
    load_u.start()
    enter(sizes)

    @pl.loop(0, hidden_blocks)
    def _(h):
        hidden_t[h] = hidden[h].T

    def term(a, j):
        if a == 0:
            return mm(hidden_t[down_rows[j]], cot[down_cols[j]], 1, 0)
        return mm(xt[up_rows[j]], pre_grad[up_cols[j]], 1, 0)

    def first_tile(q, c_of, k):
        return (q * 2 + c_of) * per + k * size

    width = 4 if size % 4 == 0 else 1

    def staged(a, k, q):
        at = (k * chips + q) * size
        return (stage if a == 0 else d_all).at[pl.ds(at, size)]

    def core_copy(a, k, q):
        return remote(
            staged(a, k, q), core_in.at[a, q, pl.ds(k * size, size)],
            cs_sem.at[a, k, q], cr_sem.at[a, k, q], {"fsdp": r * 2 + 1 - c},
        )

    def hand_over(a, k):
        for q in range(chips):
            target = staged(a, k, q)

            @pl.loop(0, size // width)
            def _(i):
                values = [term(a, first_tile(q, 1 - c, k) + i * width + w) for w in range(width)]
                for w in range(width):
                    target[i * width + w] = values[w].astype(jnp.bfloat16)

        for q in range(chips):
            core_copy(a, k, q).start()

    def sum_with(a, k, q, target, terms):
        @pl.loop(0, size // width)
        def _(i):
            values = [term(a, first_tile(q, c, k) + i * width + w) for w in range(width)]
            for w in range(width):
                total = values[w].astype(jnp.bfloat16).astype(jnp.float32)
                for other in terms:
                    total += other[i * width + w].astype(jnp.float32)
                target[i * width + w] = total.astype(jnp.bfloat16)

    def x_copy(a, k, d):
        q = lax.rem(r + d, chips)
        return remote(
            core_in.at[a, q, pl.ds(k * size, size)], x_in.at[a, d - 1, pl.ds(k * size, size)],
            xs_sem.at[a, k, d], xr_sem.at[a, k, d], {"fsdp": q * 2 + c},
        )

    def done_piece(a, k):
        return core_in.at[a, r, pl.ds(k * size, size)]

    def y_copy(a, k, e):
        return remote(
            done_piece(a, k), others[a].at[e - 1, pl.ds(k * size, size)],
            ys_sem.at[a, k, e], yr_sem.at[a, k, e], {"dp": lax.rem(y + e, replicas)},
        )

    def keep_copy(a, k):
        return pltpu.make_async_copy(
            done_piece(a, k), sums[a].at[pl.ds(k * size, size)], keep_sem.at[a, k]
        )

    def feed(a, k):
        for d in range(1, chips):
            q = lax.rem(r + d, chips)
            core_copy(a, k, q).wait_recv()
            mine = core_in.at[a, q, pl.ds(k * size, size)]
            sum_with(a, k, q, mine, [mine])
            x_copy(a, k, d).start()

    def x_event(a, k):
        core_copy(a, k, r).wait_recv()
        for d in range(1, chips):
            x_copy(a, k, d).wait_recv()
        mine = done_piece(a, k)
        sum_with(
            a, k, r, mine,
            [mine] + [x_in.at[a, d - 1, pl.ds(k * size, size)] for d in range(1, chips)],
        )
        for e in range(1, replicas):
            y_copy(a, k, e).start()
        keep_copy(a, k).start()

    def shard(ref, s):
        return ref.at[pl.ds(s * blocks, blocks)]

    def line(a, i, way, source):
        s = n - 1 - i if way > 0 else i
        k = 0 if way > 0 else 1
        src = shard(parts[a], s) if source else held[k].at[a, i]
        return remote(
            src, held[k].at[a, i], zs_sem.at[a, k, i], zr_sem.at[a, k, i], {"tensor": z + way}
        )

    def edge(way):
        return z == 0 if way > 0 else z == n - 1

    def sends(i, way):
        return n - 1 - i > z if way > 0 else i < z

    def z_start(a):
        for i in range(n - 1):
            for way in (1, -1):

                @pl.when(edge(way))
                def _():
                    line(a, i, way, True).start()

    def z_event(t, a):
        for way in (1, -1):
            i = t - z if way > 0 else t - (n - 1 - z)
            s = n - 1 - i if way > 0 else i
            k = 0 if way > 0 else 1
            on_way = jnp.logical_and(i >= 0, sends(i, way))

            @pl.when(jnp.logical_and(on_way, jnp.logical_not(edge(way))))
            def _():
                line(a, i, way, False).wait_recv()
                add_into(held[k].at[a, i], (held[k].at[a, i], shard(parts[a], s)))
                line(a, i, way, False).start()

    def slope_part(g):
        span = hidden_blocks // 4

        @pl.loop(g * span, (g + 1) * span)
        def _(h):
            first = h * COL_TILES
            value = mm(cot[df[first]], d_all[do[first]], 1, 1)
            for k in range(1, COL_TILES):
                value += mm(cot[df[first + k]], d_all[do[first + k]], 1, 1)
            pre_grad[h] = (value * slope[h]).astype(jnp.bfloat16)

    def run_part(a, g):
        order, near, fresh = (
            (far_order_d, far_near_d, far_first_d) if a == 0 else (far_order_u, far_near_u, far_first_u)
        )
        left, right, cut = (hidden, d_all, 0) if a == 0 else (pre_grad, u_all, 1)
        span = total_tiles // 4 // 8
        if g == 0:
            acc[...] = jnp.zeros_like(acc)

        @pl.loop(g * span, (g + 1) * span)
        def _(b):
            spots = [b * 8 + k for k in range(8)]
            products = [mm(left[near[i]], right[order[i]], 1, cut) for i in spots]
            total = acc[...]
            for i, product in zip(spots, products):
                total = jnp.where(fresh[i] == 1, 0.0, total) + product
                run[i] = total.astype(jnp.bfloat16)
            acc[...] = total

    def settle(a):
        last = last_d if a == 0 else last_u
        target = parts[a]

        @pl.loop(0, target.shape[0])
        def _(b):
            spot = last[b]
            found = run[jnp.maximum(spot, 0)]
            target[b] = jnp.where(spot >= 0, found, jnp.zeros_like(found))

        z_start(a)

    for k in range(PIECES):
        hand_over(0, k)
        if k >= 1:
            feed(0, k - 1)
    feed(0, PIECES - 1)
    load_d.wait()
    load_u.wait()
    work = (
        [functools.partial(slope_part, g) for g in range(4)]
        + [functools.partial(run_part, 0, g) for g in range(4)]
        + [functools.partial(settle, 0)]
        + [functools.partial(run_part, 1, g) for g in range(4)]
        + [functools.partial(settle, 1)]
    )
    slots = [(t, a) for a in range(2) for t in range(1, n - 1)]
    pieces = [(a, k) for a in range(2) for k in range(PIECES)]
    handed = 0
    fed = 0
    for i, piece in enumerate(pieces):
        for step in work[:3]:
            step()
        work = work[3:]
        if not work:
            for _ in range(2):
                if handed < PIECES:
                    hand_over(1, handed)
                    handed += 1
            for _ in range(2):
                if fed < handed - 1 or fed < handed == PIECES:
                    feed(1, fed)
                    fed += 1
        if i in (5, 7, 11, 13) and slots:
            z_event(*slots.pop(0))
        x_event(*piece)
    for slot in slots:
        z_event(*slot)

    for a in range(2):
        mine = shard(parts[a], z)

        @pl.when(z > 0)
        def _():
            line(a, n - 1 - z, 1, False).wait_recv()

        @pl.when(z < n - 1)
        def _():
            line(a, z, -1, False).wait_recv()

        @pl.when(z == 0)
        def _():
            add_into(outs[a], (mine, held_l.at[a, z]))

        @pl.when(z == n - 1)
        def _():
            add_into(outs[a], (mine, held_r.at[a, n - 1 - z]))

        @pl.when(jnp.logical_and(z > 0, z < n - 1))
        def _():
            add_into(outs[a], (mine, held_r.at[a, n - 1 - z], held_l.at[a, z]))

        for i in range(n - 1):
            for way in (1, -1):

                @pl.when(sends(i, way))
                def _():
                    line(a, i, way, False).wait_send()

        for k in range(PIECES):
            for q in range(chips):
                core_copy(a, k, q).wait_send()
            for d in range(1, chips):
                x_copy(a, k, d).wait_send()
            keep_copy(a, k).wait()
            for e in range(1, replicas):
                y_copy(a, k, e).wait()


def reduce(sizes, tables, hidden, slope, xt, cot, up, down):
    n, chips, replicas = sizes
    blocks = cot.shape[0] // n
    rows = cot.shape[1]
    per = up.shape[0] // (2 * chips)
    kind = jnp.bfloat16
    dma = pltpu.SemaphoreType.DMA
    vmem = pl.BlockSpec(memory_space=pltpu.VMEM)
    smem = pl.BlockSpec(memory_space=pltpu.SMEM)
    anywhere = pl.BlockSpec(memory_space=pl.ANY)
    return pl.pallas_call(
        functools.partial(reduce_kernel, sizes),
        out_shape=(
            [jax.ShapeDtypeStruct((blocks, rows, 128), kind)] * 2
            + [jax.ShapeDtypeStruct((per, 128, 128), kind)] * 2
            + [jax.ShapeDtypeStruct((replicas - 1, per, 128, 128), kind)] * 2
        ),
        in_specs=[smem] * len(tables) + [vmem] * 4 + [anywhere] * 2,
        out_specs=[vmem] * 2 + [anywhere] * 4,
        scratch_shapes=[
            pltpu.VMEM(up.shape, kind),
            pltpu.VMEM(down.shape, kind),
            pltpu.VMEM((hidden.shape[0], 128, rows), kind),
            pltpu.VMEM(hidden.shape, kind),
            pltpu.VMEM((up.shape[0], rows, 128), kind),
            pltpu.VMEM((rows, 128), jnp.float32),
            pltpu.VMEM(cot.shape, kind),
            pltpu.VMEM(cot.shape, kind),
            pltpu.VMEM((2, n - 1, blocks, rows, 128), kind),
            pltpu.VMEM((2, n - 1, blocks, rows, 128), kind),
            pltpu.VMEM((chips * per, 128, 128), kind),
            pltpu.VMEM((2, chips, per, 128, 128), kind),
            pltpu.VMEM((2, max(chips - 1, 1), per, 128, 128), kind),
            dma((2,)),
            dma((2, PIECES)),
            dma((2, 2, n)),
            dma((2, 2, n)),
            dma((2, PIECES, chips)),
            dma((2, PIECES, chips)),
            dma((2, PIECES, chips)),
            dma((2, PIECES, chips)),
            dma((2, PIECES, replicas)),
            dma((2, PIECES, replicas)),
        ],
        compiler_params=pltpu.CompilerParams(
            collective_id=1, has_side_effects=True, vmem_limit_bytes=67043328
        ),
        name="reduce_all",
    )(*tables, hidden, slope, xt, cot, up, down)


def tables_of(near, far, model_blocks):
    count = near.shape[0]
    at = lax.iota(jnp.int32, count)
    before = at[:, None] < at[None, :]
    equal = far[:, None] == far[None, :]
    spot = near * COL_TILES + jnp.sum(((near[:, None] == near[None, :]) & before).astype(jnp.int32), axis=0)
    here = spot[:, None] == at[None, :]
    packed = jnp.sum(jnp.where(here, (at * model_blocks + far)[:, None], 0), axis=0)
    rank = jnp.sum((equal & before).astype(jnp.int32), axis=0)
    place_of = rank + jnp.sum((far[:, None] < far[None, :]).astype(jnp.int32), axis=0)
    there = place_of[:, None] == at[None, :]
    code = (at * count + near) * 2 + (rank == 0)
    far_packed = jnp.sum(jnp.where(there, code[:, None], 0), axis=0)
    block = lax.iota(jnp.int32, model_blocks)
    matches = far[:, None] == block[None, :]
    until = jnp.sum((far[:, None] <= block[None, :]).astype(jnp.int32), axis=0)
    last = jnp.where(jnp.any(matches, axis=0), until - 1, -1)
    far_code = far_packed // 2
    return (
        packed // model_blocks, packed % model_blocks,
        far_code // count, far_code % count, far_packed % 2, last,
    )


def body(sizes, activations, cotangent, up_tiles, down_tiles, up_rows, up_cols, down_rows, down_cols):
    ur, uc, dr, dc = (v[:, 0] for v in (up_rows, up_cols, down_rows, down_cols))
    model_blocks = sizes[0] * activations.shape[1] // 128
    sort = jax.vmap(functools.partial(tables_of, model_blocks=model_blocks))
    order, far, far_order, far_near, far_first, last = sort(jnp.stack([uc, dr]), jnp.stack([ur, dc]))
    cot, up, down, hidden, slope, xt = gather(
        sizes, order[0], far[0], activations, cotangent, up_tiles, down_tiles
    )
    tables = (
        order[1], far[1], ur, uc, dr, dc,
        far_order[0], far_near[0], far_first[0], last[0],
        far_order[1], far_near[1], far_first[1], last[1],
    )
    out, inp, ga_u, ga_d, gb_u, gb_d = reduce(sizes, tables, hidden, slope, xt, cot, up, down)

    def flat(v):
        return v.transpose(1, 0, 2).reshape(v.shape[1], -1)

    def total(a, b):
        return a.astype(jnp.float32) + jnp.sum(b.astype(jnp.float32), axis=0)

    return flat(out), flat(inp), total(ga_u, gb_u), total(ga_d, gb_d)


def solution(mesh):
    sizes = (mesh.shape["tensor"], mesh.shape["fsdp"] // 2, mesh.shape["dp"])
    in_specs = (
        P(("dp", "fsdp"), "tensor"),
        P(("dp", "fsdp"), "tensor"),
        P(("fsdp", "tensor"), None, None),
        P(("fsdp", "tensor"), None, None),
        P(None, "tensor"),
        P(None, "tensor"),
        P(None, "tensor"),
        P(None, "tensor"),
    )
    out_specs = (
        P(("dp", "fsdp"), "tensor"),
        P(("dp", "fsdp"), "tensor"),
        P(("fsdp", "tensor"), None, None),
        P(("fsdp", "tensor"), None, None),
    )
    return jax.shard_map(
        functools.partial(body, sizes), mesh=mesh, in_specs=in_specs, out_specs=out_specs,
        check_vma=False,
    )
```

```python
import functools

import jax
import jax.numpy as jnp
from jax import lax
from jax.experimental import pallas as pl
from jax.experimental.pallas import tpu as pltpu
from jax.sharding import PartitionSpec as P

MESH = pl.DeviceIdType.MESH
COL_TILES = 8
PIECES = 8

inv_root_two = 0.7071067811865476
inv_root_tau = 0.3989422804014327


def gelu_parts(values):
    normal_cdf = 0.5 * (1.0 + lax.erf(values * inv_root_two))
    density = inv_root_tau * jnp.exp(-0.5 * values * values)
    return (values * normal_cdf, normal_cdf + values * density)


def remote(src, dst, send_sem, recv_sem, where):
    return pltpu.make_async_remote_copy(
        src_ref=src, dst_ref=dst, send_sem=send_sem, recv_sem=recv_sem,
        device_id=where, device_id_type=MESH,
    )


def place(sizes):
    n, chips, replicas = sizes
    z = lax.axis_index("tensor")
    f = lax.axis_index("fsdp")
    y = lax.axis_index("dp")
    return z, f // 2, f % 2, y


def enter(sizes):
    n, chips, replicas = sizes
    z, r, c, y = place(sizes)
    barrier = pltpu.get_barrier_semaphore()

    def greet(where):
        pl.semaphore_signal(barrier, inc=1, device_id=where, device_id_type=MESH)

    @pl.when(z < n - 1)
    def _():
        greet({"tensor": z + 1})

    @pl.when(z > 0)
    def _():
        greet({"tensor": z - 1})

    greet({"fsdp": r * 2 + 1 - c})
    for d in range(1, chips):
        greet({"fsdp": lax.rem(r + d, chips) * 2 + c})
    for e in range(1, replicas):
        greet({"dp": lax.rem(y + e, replicas)})
    sides = jnp.where(z < n - 1, 1, 0) + jnp.where(z > 0, 1, 0)
    pl.semaphore_wait(barrier, sides + 1 + (chips - 1) + (replicas - 1))


def gather_kernel(
    sizes, uo, uf, act, cot, up, down, c_all, u_all, d_all, hidden, slope, xt,
    x_all, u_held, own_c, own_u, own_d,
    load_sem, keep_sem, zs_sem, zr_sem, xs_sem, xr_sem, ys_sem, yr_sem, cs_sem, cr_sem,
):
    n, chips, replicas = sizes
    z, r, c, y = place(sizes)
    f = r * 2 + c
    blocks = own_c.shape[0]
    per = up.shape[0]
    part = per // replicas
    own_x = x_all.at[pl.ds(z * blocks, blocks)]
    features = ((act, own_x, x_all), (cot, own_c, c_all))
    weights = ((up, own_u, u_all), (down, own_d, d_all))

    loads = []
    for a, (src, own, _) in enumerate(features):
        for b in range(blocks):
            copy = pltpu.make_async_copy(
                src.at[:, pl.ds(b * 128, 128)], own.at[b], load_sem.at[a, b]
            )
            copy.start()
            loads.append(copy)
    for a, (src, own, _) in enumerate(weights):
        copy = pltpu.make_async_copy(src, own, load_sem.at[2 + a, 0])
        copy.start()
    enter(sizes)
    for copy in loads:
        copy.wait()

    def shard(full, s):
        return full.at[pl.ds(s * blocks, blocks)]

    def line(a, s, way, source):
        _, own, full = features[a]
        k = 0 if way > 0 else 1
        mine = own if source else shard(full, z - way * s)
        return remote(
            mine, shard(full, z - way * s), zs_sem.at[a, k, s], zr_sem.at[a, k, s],
            {"tensor": z + way},
        )

    def can_send(way):
        return z < n - 1 if way > 0 else z > 0

    def has(s, way):
        return z - s >= 0 if way > 0 else z + s <= n - 1

    def z_start(a):
        for way in (1, -1):

            @pl.when(can_send(way))
            def _():
                line(a, 0, way, True).start()

    z_start(0)

    def tile_range(full, r_of, c_of, q):
        return full.at[pl.ds((r_of * 2 + c_of) * per + q * part, part)]

    def x_copy(a, d):
        src = weights[a][0].at[pl.ds(y * part, part)]
        return remote(
            src, tile_range(weights[a][2], r, c, y), xs_sem.at[a, d], xr_sem.at[a, d],
            {"fsdp": lax.rem(r + d, chips) * 2 + c},
        )

    for a in range(2):
        for d in range(1, chips):
            x_copy(a, d).start()

    def own_core(a):
        full = weights[a][2]
        return remote(
            weights[a][0], full.at[pl.ds(f * per, per)], cs_sem.at[a, 0, 0], cr_sem.at[a, 0, 0],
            {"fsdp": r * 2 + 1 - c},
        )

    for a in range(2):
        own_core(a).start()

    keeps = []
    keeps.append(pltpu.make_async_copy(own_c, shard(c_all, z), keep_sem.at[0]))
    for a, (src, own, full) in enumerate(weights):
        pltpu.make_async_copy(src, own, load_sem.at[2 + a, 0]).wait()
        keeps.append(
            pltpu.make_async_copy(own, full.at[pl.ds(f * per, per)], keep_sem.at[1 + a])
        )
    for copy in keeps:
        copy.start()

    def y_copy(a, d, e):
        piece = tile_range(weights[a][2], lax.rem(r - d + chips, chips), c, y)
        return remote(
            piece, piece, ys_sem.at[a, d, e], yr_sem.at[a, d, e],
            {"dp": lax.rem(y + e, replicas)},
        )

    def core_copy(a, d, e):
        q = lax.rem(y - e + replicas, replicas)
        piece = tile_range(weights[a][2], lax.rem(r - d + chips, chips), c, q)
        return remote(
            piece, piece, cs_sem.at[a, d, e], cr_sem.at[a, d, e], {"fsdp": r * 2 + 1 - c}
        )

    def z_event(a, s):
        for way in (1, -1):

            @pl.when(has(s, way))
            def _():
                line(a, s - 1, way, False).wait_recv()

                if s < n - 1:

                    @pl.when(can_send(way))
                    def _():
                        line(a, s, way, False).start()

    def x_event(a):
        for d in range(1, chips):
            x_copy(a, d).wait_recv()
            for e in range(1, replicas):
                y_copy(a, d, e).start()
            core_copy(a, d, 0).start()

    def y_event(a):
        for d in range(1, chips):
            for e in range(1, replicas):
                y_copy(a, d, e).wait_recv()
                core_copy(a, d, e).start()

    load_up = pltpu.make_async_copy(u_all, u_held, load_sem.at[4, 0])

    def fetch_up():
        keeps[1].wait()
        own_core(0).wait_recv()
        for d in range(1, chips):
            for e in range(replicas):
                core_copy(0, d, e).wait_recv()
        load_up.start()
        load_up.wait()

    def turn():
        @pl.loop(0, x_all.shape[0])
        def _(b):
            xt[b] = x_all[b].T

    hidden_blocks = hidden.shape[0]

    def forward_part(g):
        span = hidden_blocks // 4

        @pl.loop(g * span, (g + 1) * span)
        def _(h):
            first = h * COL_TILES
            pre = mm(x_all[uf[first]], u_held[uo[first]], 1, 0)
            for k in range(1, COL_TILES):
                pre += mm(x_all[uf[first + k]], u_held[uo[first + k]], 1, 0)
            value, tangent = gelu_parts(pre)
            hidden[h] = value.astype(jnp.bfloat16)
            slope[h] = tangent

    for s in range(1, n - 1):
        z_event(0, s)
    z_start(1)
    x_event(0)
    z_event(0, n - 1)
    turn()
    x_event(1)
    y_event(0)
    later = [functools.partial(z_event, 1, s) for s in range(1, n - 1)]
    later.pop(0)()
    fetch_up()
    forward_part(0)
    forward_part(1)
    for event in later:
        event()
    forward_part(2)
    y_event(1)
    forward_part(3)
    z_event(1, n - 1)

    keeps[0].wait()
    keeps[2].wait()
    own_core(1).wait_recv()
    for a in range(2):
        own_core(a).wait_send()
        for d in range(1, chips):
            x_copy(a, d).wait_send()
            for e in range(replicas):
                core_copy(a, d, e).wait_send()
                if a == 1:
                    core_copy(a, d, e).wait_recv()
            for e in range(1, replicas):
                y_copy(a, d, e).wait_send()
        for way in (1, -1):
            for s in range(n - 1):

                @pl.when(jnp.logical_and(can_send(way), has(s, way)))
                def _():
                    line(a, s, way, s == 0).wait_send()


def gather(sizes, order, far, activations, cotangent, up_tiles, down_tiles):
    n, chips, replicas = sizes
    rows, wide = activations.shape
    blocks = wide // 128
    per = up_tiles.shape[0]
    hidden_blocks = 2 * chips * per // COL_TILES
    kind = jnp.bfloat16
    dma = pltpu.SemaphoreType.DMA
    vmem = pl.BlockSpec(memory_space=pltpu.VMEM)
    smem = pl.BlockSpec(memory_space=pltpu.SMEM)
    anywhere = pl.BlockSpec(memory_space=pl.ANY)
    return pl.pallas_call(
        functools.partial(gather_kernel, sizes),
        out_shape=(
            jax.ShapeDtypeStruct((n * blocks, rows, 128), kind),
            jax.ShapeDtypeStruct((2 * chips * per, 128, 128), kind),
            jax.ShapeDtypeStruct((2 * chips * per, 128, 128), kind),
            jax.ShapeDtypeStruct((hidden_blocks, rows, 128), kind),
            jax.ShapeDtypeStruct((hidden_blocks, rows, 128), jnp.float32),
            jax.ShapeDtypeStruct((n * blocks, 128, rows), kind),
        ),
        in_specs=[smem] * 2 + [anywhere] * 4,
        out_specs=(anywhere,) * 3 + (vmem,) * 3,
        scratch_shapes=[
            pltpu.VMEM((n * blocks, rows, 128), kind),
            pltpu.VMEM((2 * chips * per, 128, 128), kind),
            pltpu.VMEM((blocks, rows, 128), kind),
            pltpu.VMEM((per, 128, 128), kind),
            pltpu.VMEM((per, 128, 128), kind),
            dma((5, blocks)),
            dma((3,)),
            dma((2, 2, n)),
            dma((2, 2, n)),
            dma((2, chips)),
            dma((2, chips)),
            dma((2, chips, replicas)),
            dma((2, chips, replicas)),
            dma((2, chips, replicas)),
            dma((2, chips, replicas)),
        ],
        compiler_params=pltpu.CompilerParams(
            collective_id=0, has_side_effects=True, vmem_limit_bytes=60 * 1024 * 1024
        ),
        name="gather_all",
    )(order, far, activations, cotangent, up_tiles, down_tiles)


def mm(a, b, ca, cb):
    return lax.dot_general(a, b, (((ca,), (cb,)), ((), ())), preferred_element_type=jnp.float32)


def add_into(target, terms):
    @pl.loop(0, target.shape[0])
    def _(b):
        total = terms[0][b].astype(jnp.float32)
        for term in terms[1:]:
            total += term[b].astype(jnp.float32)
        target[b] = total.astype(target.dtype)


def reduce_kernel(
    sizes, do, df, up_rows, up_cols, down_rows, down_cols,
    far_order_u, far_near_u, far_first_u, last_u, far_order_d, far_near_d, far_first_d, last_d,
    hidden, slope, xt, cot, up, down,
    out, inp, ga_u, ga_d, gb_u, gb_d,
    u_all, d_all, hidden_t, pre_grad, run, acc, parts_o, parts_i,
    held_r, held_l, stage, core_in, x_in,
    load_sem, keep_sem, zs_sem, zr_sem, cs_sem, cr_sem, xs_sem, xr_sem, ys_sem, yr_sem,
):
    n, chips, replicas = sizes
    z, r, c, y = place(sizes)
    blocks = out.shape[0]
    hidden_blocks = hidden.shape[0]
    per = ga_u.shape[0]
    total_tiles = u_all.shape[0]
    size = per // PIECES
    parts = (parts_o, parts_i)
    outs = (out, inp)
    sums = (ga_d, ga_u)
    others = (gb_d, gb_u)
    held = (held_r, held_l)

    load_d = pltpu.make_async_copy(down, d_all, load_sem.at[0])
    load_u = pltpu.make_async_copy(up, u_all, load_sem.at[1])
    load_d.start()
    load_u.start()
    enter(sizes)

    @pl.loop(0, hidden_blocks)
    def _(h):
        hidden_t[h] = hidden[h].T

    def term(a, j):
        if a == 0:
            return mm(hidden_t[down_rows[j]], cot[down_cols[j]], 1, 0)
        return mm(xt[up_rows[j]], pre_grad[up_cols[j]], 1, 0)

    def first_tile(q, c_of, k):
        return (q * 2 + c_of) * per + k * size

    width = 4 if size % 4 == 0 else 1

    def staged(a, k, q):
        at = (k * chips + q) * size
        return (stage if a == 0 else d_all).at[pl.ds(at, size)]

    def core_copy(a, k, q):
        return remote(
            staged(a, k, q), core_in.at[a, q, pl.ds(k * size, size)],
            cs_sem.at[a, k, q], cr_sem.at[a, k, q], {"fsdp": r * 2 + 1 - c},
        )

    def hand_over(a, k):
        for q in range(chips):
            target = staged(a, k, q)

            @pl.loop(0, size // width)
            def _(i):
                values = [term(a, first_tile(q, 1 - c, k) + i * width + w) for w in range(width)]
                for w in range(width):
                    target[i * width + w] = values[w].astype(jnp.bfloat16)

        for q in range(chips):
            core_copy(a, k, q).start()

    def sum_with(a, k, q, target, terms):
        @pl.loop(0, size // width)
        def _(i):
            values = [term(a, first_tile(q, c, k) + i * width + w) for w in range(width)]
            for w in range(width):
                total = values[w].astype(jnp.bfloat16).astype(jnp.float32)
                for other in terms:
                    total += other[i * width + w].astype(jnp.float32)
                target[i * width + w] = total.astype(jnp.bfloat16)

    def x_copy(a, k, d):
        q = lax.rem(r + d, chips)
        return remote(
            core_in.at[a, q, pl.ds(k * size, size)], x_in.at[a, d - 1, pl.ds(k * size, size)],
            xs_sem.at[a, k, d], xr_sem.at[a, k, d], {"fsdp": q * 2 + c},
        )

    def done_piece(a, k):
        return core_in.at[a, r, pl.ds(k * size, size)]

    def y_copy(a, k, e):
        return remote(
            done_piece(a, k), others[a].at[e - 1, pl.ds(k * size, size)],
            ys_sem.at[a, k, e], yr_sem.at[a, k, e], {"dp": lax.rem(y + e, replicas)},
        )

    def keep_copy(a, k):
        return pltpu.make_async_copy(
            done_piece(a, k), sums[a].at[pl.ds(k * size, size)], keep_sem.at[a, k]
        )

    def feed(a, k):
        for d in range(1, chips):
            q = lax.rem(r + d, chips)
            core_copy(a, k, q).wait_recv()
            mine = core_in.at[a, q, pl.ds(k * size, size)]
            sum_with(a, k, q, mine, [mine])
            x_copy(a, k, d).start()

    def x_event(a, k):
        core_copy(a, k, r).wait_recv()
        for d in range(1, chips):
            x_copy(a, k, d).wait_recv()
        mine = done_piece(a, k)
        sum_with(
            a, k, r, mine,
            [mine] + [x_in.at[a, d - 1, pl.ds(k * size, size)] for d in range(1, chips)],
        )
        for e in range(1, replicas):
            y_copy(a, k, e).start()
        keep_copy(a, k).start()

    def shard(ref, s):
        return ref.at[pl.ds(s * blocks, blocks)]

    def line(a, i, way, source):
        s = n - 1 - i if way > 0 else i
        k = 0 if way > 0 else 1
        src = shard(parts[a], s) if source else held[k].at[a, i]
        return remote(
            src, held[k].at[a, i], zs_sem.at[a, k, i], zr_sem.at[a, k, i], {"tensor": z + way}
        )

    def edge(way):
        return z == 0 if way > 0 else z == n - 1

    def sends(i, way):
        return n - 1 - i > z if way > 0 else i < z

    def z_start(a):
        for i in range(n - 1):
            for way in (1, -1):

                @pl.when(edge(way))
                def _():
                    line(a, i, way, True).start()

    def z_event(t, a):
        for way in (1, -1):
            i = t - z if way > 0 else t - (n - 1 - z)
            s = n - 1 - i if way > 0 else i
            k = 0 if way > 0 else 1
            on_way = jnp.logical_and(i >= 0, sends(i, way))

            @pl.when(jnp.logical_and(on_way, jnp.logical_not(edge(way))))
            def _():
                line(a, i, way, False).wait_recv()
                add_into(held[k].at[a, i], (held[k].at[a, i], shard(parts[a], s)))
                line(a, i, way, False).start()

    def slope_part(g):
        span = hidden_blocks // 4

        @pl.loop(g * span, (g + 1) * span)
        def _(h):
            first = h * COL_TILES
            value = mm(cot[df[first]], d_all[do[first]], 1, 1)
            for k in range(1, COL_TILES):
                value += mm(cot[df[first + k]], d_all[do[first + k]], 1, 1)
            pre_grad[h] = (value * slope[h]).astype(jnp.bfloat16)

    def run_part(a, g):
        order, near, fresh = (
            (far_order_d, far_near_d, far_first_d) if a == 0 else (far_order_u, far_near_u, far_first_u)
        )
        left, right, cut = (hidden, d_all, 0) if a == 0 else (pre_grad, u_all, 1)
        span = total_tiles // 4 // 8
        if g == 0:
            acc[...] = jnp.zeros_like(acc)

        @pl.loop(g * span, (g + 1) * span)
        def _(b):
            spots = [b * 8 + k for k in range(8)]
            products = [mm(left[near[i]], right[order[i]], 1, cut) for i in spots]
            total = acc[...]
            for i, product in zip(spots, products):
                total = jnp.where(fresh[i] == 1, 0.0, total) + product
                run[i] = total.astype(jnp.bfloat16)
            acc[...] = total

    def settle(a):
        last = last_d if a == 0 else last_u
        target = parts[a]

        @pl.loop(0, target.shape[0])
        def _(b):
            spot = last[b]
            found = run[jnp.maximum(spot, 0)]
            target[b] = jnp.where(spot >= 0, found, jnp.zeros_like(found))

        z_start(a)

    for k in range(PIECES):
        hand_over(0, k)
        if k >= 1:
            feed(0, k - 1)
    feed(0, PIECES - 1)
    load_d.wait()
    load_u.wait()
    work = (
        [functools.partial(slope_part, g) for g in range(4)]
        + [functools.partial(run_part, 0, g) for g in range(4)]
        + [functools.partial(settle, 0)]
        + [functools.partial(run_part, 1, g) for g in range(4)]
        + [functools.partial(settle, 1)]
    )
    slots = [(t, a) for a in range(2) for t in range(1, n - 1)]
    pieces = [(a, k) for a in range(2) for k in range(PIECES)]
    handed = 0
    fed = 0
    for i, piece in enumerate(pieces):
        for step in work[:5]:
            step()
        work = work[5:]
        if not work:
            for _ in range(2):
                if handed < PIECES:
                    hand_over(1, handed)
                    handed += 1
            for _ in range(2):
                if fed < handed - 1 or fed < handed == PIECES:
                    feed(1, fed)
                    fed += 1
        if i in (4, 6, 10, 12) and slots:
            z_event(*slots.pop(0))
        x_event(*piece)
    for slot in slots:
        z_event(*slot)

    for a in range(2):
        mine = shard(parts[a], z)

        @pl.when(z > 0)
        def _():
            line(a, n - 1 - z, 1, False).wait_recv()

        @pl.when(z < n - 1)
        def _():
            line(a, z, -1, False).wait_recv()

        @pl.when(z == 0)
        def _():
            add_into(outs[a], (mine, held_l.at[a, z]))

        @pl.when(z == n - 1)
        def _():
            add_into(outs[a], (mine, held_r.at[a, n - 1 - z]))

        @pl.when(jnp.logical_and(z > 0, z < n - 1))
        def _():
            add_into(outs[a], (mine, held_r.at[a, n - 1 - z], held_l.at[a, z]))

        for i in range(n - 1):
            for way in (1, -1):

                @pl.when(sends(i, way))
                def _():
                    line(a, i, way, False).wait_send()

        for k in range(PIECES):
            for q in range(chips):
                core_copy(a, k, q).wait_send()
            for d in range(1, chips):
                x_copy(a, k, d).wait_send()
            keep_copy(a, k).wait()
            for e in range(1, replicas):
                y_copy(a, k, e).wait()


def reduce(sizes, tables, hidden, slope, xt, cot, up, down):
    n, chips, replicas = sizes
    blocks = cot.shape[0] // n
    rows = cot.shape[1]
    per = up.shape[0] // (2 * chips)
    kind = jnp.bfloat16
    dma = pltpu.SemaphoreType.DMA
    vmem = pl.BlockSpec(memory_space=pltpu.VMEM)
    smem = pl.BlockSpec(memory_space=pltpu.SMEM)
    anywhere = pl.BlockSpec(memory_space=pl.ANY)
    return pl.pallas_call(
        functools.partial(reduce_kernel, sizes),
        out_shape=(
            [jax.ShapeDtypeStruct((blocks, rows, 128), kind)] * 2
            + [jax.ShapeDtypeStruct((per, 128, 128), kind)] * 2
            + [jax.ShapeDtypeStruct((replicas - 1, per, 128, 128), kind)] * 2
        ),
        in_specs=[smem] * len(tables) + [vmem] * 4 + [anywhere] * 2,
        out_specs=[vmem] * 2 + [anywhere] * 4,
        scratch_shapes=[
            pltpu.VMEM(up.shape, kind),
            pltpu.VMEM(down.shape, kind),
            pltpu.VMEM((hidden.shape[0], 128, rows), kind),
            pltpu.VMEM(hidden.shape, kind),
            pltpu.VMEM((up.shape[0], rows, 128), kind),
            pltpu.VMEM((rows, 128), jnp.float32),
            pltpu.VMEM(cot.shape, kind),
            pltpu.VMEM(cot.shape, kind),
            pltpu.VMEM((2, n - 1, blocks, rows, 128), kind),
            pltpu.VMEM((2, n - 1, blocks, rows, 128), kind),
            pltpu.VMEM((chips * per, 128, 128), kind),
            pltpu.VMEM((2, chips, per, 128, 128), kind),
            pltpu.VMEM((2, max(chips - 1, 1), per, 128, 128), kind),
            dma((2,)),
            dma((2, PIECES)),
            dma((2, 2, n)),
            dma((2, 2, n)),
            dma((2, PIECES, chips)),
            dma((2, PIECES, chips)),
            dma((2, PIECES, chips)),
            dma((2, PIECES, chips)),
            dma((2, PIECES, replicas)),
            dma((2, PIECES, replicas)),
        ],
        compiler_params=pltpu.CompilerParams(
            collective_id=1, has_side_effects=True, vmem_limit_bytes=67043328
        ),
        name="reduce_all",
    )(*tables, hidden, slope, xt, cot, up, down)


def tables_of(near, far, model_blocks):
    count = near.shape[0]
    at = lax.iota(jnp.int32, count)
    before = at[:, None] < at[None, :]
    equal = far[:, None] == far[None, :]
    spot = near * COL_TILES + jnp.sum(((near[:, None] == near[None, :]) & before).astype(jnp.int32), axis=0)
    here = spot[:, None] == at[None, :]
    packed = jnp.sum(jnp.where(here, (at * model_blocks + far)[:, None], 0), axis=0)
    rank = jnp.sum((equal & before).astype(jnp.int32), axis=0)
    place_of = rank + jnp.sum((far[:, None] < far[None, :]).astype(jnp.int32), axis=0)
    there = place_of[:, None] == at[None, :]
    code = (at * count + near) * 2 + (rank == 0)
    far_packed = jnp.sum(jnp.where(there, code[:, None], 0), axis=0)
    block = lax.iota(jnp.int32, model_blocks)
    matches = far[:, None] == block[None, :]
    until = jnp.sum((far[:, None] <= block[None, :]).astype(jnp.int32), axis=0)
    last = jnp.where(jnp.any(matches, axis=0), until - 1, -1)
    far_code = far_packed // 2
    return (
        packed // model_blocks, packed % model_blocks,
        far_code // count, far_code % count, far_packed % 2, last,
    )


def body(sizes, activations, cotangent, up_tiles, down_tiles, up_rows, up_cols, down_rows, down_cols):
    ur, uc, dr, dc = (v[:, 0] for v in (up_rows, up_cols, down_rows, down_cols))
    model_blocks = sizes[0] * activations.shape[1] // 128
    sort = jax.vmap(functools.partial(tables_of, model_blocks=model_blocks))
    order, far, far_order, far_near, far_first, last = sort(jnp.stack([uc, dr]), jnp.stack([ur, dc]))
    cot, up, down, hidden, slope, xt = gather(
        sizes, order[0], far[0], activations, cotangent, up_tiles, down_tiles
    )
    tables = (
        order[1], far[1], ur, uc, dr, dc,
        far_order[0], far_near[0], far_first[0], last[0],
        far_order[1], far_near[1], far_first[1], last[1],
    )
    out, inp, ga_u, ga_d, gb_u, gb_d = reduce(sizes, tables, hidden, slope, xt, cot, up, down)

    def flat(v):
        return v.transpose(1, 0, 2).reshape(v.shape[1], -1)

    def total(a, b):
        return a.astype(jnp.float32) + jnp.sum(b.astype(jnp.float32), axis=0)

    return flat(out), flat(inp), total(ga_u, gb_u), total(ga_d, gb_d)


def solution(mesh):
    sizes = (mesh.shape["tensor"], mesh.shape["fsdp"] // 2, mesh.shape["dp"])
    in_specs = (
        P(("dp", "fsdp"), "tensor"),
        P(("dp", "fsdp"), "tensor"),
        P(("fsdp", "tensor"), None, None),
        P(("fsdp", "tensor"), None, None),
        P(None, "tensor"),
        P(None, "tensor"),
        P(None, "tensor"),
        P(None, "tensor"),
    )
    out_specs = (
        P(("dp", "fsdp"), "tensor"),
        P(("dp", "fsdp"), "tensor"),
        P(("fsdp", "tensor"), None, None),
        P(("fsdp", "tensor"), None, None),
    )
    return jax.shard_map(
        functools.partial(body, sizes), mesh=mesh, in_specs=in_specs, out_specs=out_specs,
        check_vma=False,
    )
```
